128 devices in a mesh: ctx: 16 (over z, y), head: 8 (over x, core).
Axes of the slice: x: 4, y: 4, z: 4, core: 2. Of those that a mesh axis runs over, the one named last changes fastest.
Arguments:
- queries: bfloat16 [8192, 8192], P('ctx', 'head'), may hold values from -6 to 6
- keys: bfloat16 [8192, 8192], P('ctx', 'head'), may hold values from -6 to 6
- values: bfloat16 [8192, 8192], P('ctx', 'head'), may hold values from -6 to 6
- teacher: bfloat16 [8192, 5120], P('ctx', 'head'), may hold values from -6 to 6
- out_weight: bfloat16 [8192, 5120], P('head'), may hold values from -0.0625 to 0.0625
- valid: int32 [8192], P('ctx'), may hold values from 0 to 1, as said below
Outputs:
- q_grad: float32 [8192, 8192], P('ctx', 'head')
- k_grad: float32 [8192, 8192], P('ctx', 'head')
- v_grad: float32 [8192, 8192], P('ctx', 'head')
The draws below stay inside these ranges and needn't reach their ends.
Inputs may be any that keep to these rules, and one draw needn't show every extreme that they name: The last token always has valid = 1.
All inputs are finite; a program needn't handle non-finite values.
Results may differ from the reference program's by a relative error of at most 0.012.
Values may be sent and summed in bfloat16 or wider, within the bound.
A program may use at most 128 MiB of HBM per device.

```python
import math
import jax
import jax.numpy as jnp
from jax import lax

H = 64
DH = 128
DM = 5120
HEADS_DEV = 8
TOKENS = 8192
N_HEAD = 8


def draw_valid(key, part):
    position = jnp.arange(TOKENS, dtype=jnp.int32)
    threshold = 256 + 512 * position // TOKENS
    rolled = jax.random.randint(jax.random.fold_in(key, 7), (TOKENS,), 0, 1024, dtype=jnp.int32)
    chosen = (rolled < threshold) | (position == TOKENS - 1)
    return jnp.where(chosen, 1, 0).astype(jnp.int32)


def level_of(own_key, shape, shards, low, top_value):
    def one(dim, blocks):
        steps = jax.random.uniform(jax.random.fold_in(jax.random.fold_in(own_key, 6), dim), (blocks,), jnp.float32, low / len(shards), top_value / len(shards))
        return jnp.repeat(jnp.exp(steps), shape[dim] // blocks).reshape((-1,) + (1,) * (len(shape) - dim - 1))

    level = one(*shards[0])
    for cut in shards[1:]:
        level = level * one(*cut)
    return level


def noise(key, dims, deviation, limit, shards=(), held_as=jnp.bfloat16):
    array = jax.random.normal(key, dims, jnp.float32) * deviation
    if len(shards) > 0:
        array = level_of(key, dims, shards, -0.22, 0.18) * array
    return jnp.clip(array, min=-limit, max=limit).astype(held_as)


def setup_inputs(seed: int = 0) -> dict:
    streams_of = jax.random.split(jax.random.key(seed), 7)
    queries = noise(streams_of[0], (TOKENS, H * DH), 1.0, 6.0, ((0, 16), (1, 8)))
    keys = noise(streams_of[1], (TOKENS, H * DH), 1.0, 6.0, ((0, 16), (1, 8)))
    values = noise(streams_of[2], (TOKENS, H * DH), 1.0, 6.0, ((0, 16), (1, 8)))
    teacher = noise(streams_of[3], (TOKENS, DM), 1.0, 6.0, ((0, 16), (1, 8)))
    out_weight = noise(streams_of[4], (H * DH, DM), (H * DH) ** -0.5, 0.0625, ((0, 8),))
    valid = draw_valid(jax.random.fold_in(streams_of[6], 71), 0)
    return dict(queries=queries, keys=keys, values=values, teacher=teacher, out_weight=out_weight, valid=valid)


def reference(queries, keys, values, teacher, out_weight, valid):
    precise = lax.Precision.HIGHEST
    attn_scale = 1.0 / math.sqrt(DH * TOKENS)
    blk_rows = math.gcd(TOKENS, 512)
    blk_count = TOKENS // blk_rows
    causal = jnp.tril(jnp.ones((blk_rows, blk_rows), jnp.float32))

    def attend(query_f, key_f, value_f):
        query_blk = query_f.reshape(blk_count, blk_rows, H, DH)
        key_blk = key_f.reshape(blk_count, blk_rows, H, DH)
        value_blk = value_f.reshape(blk_count, blk_rows, H, DH)

        def block_step(kv_state, inputs):
            query_one, key_one, value_one = inputs
            scores = jnp.einsum('thd,shd->hts', query_one, key_one, precision=precise) * causal
            output = jnp.einsum('hts,she->the', scores, value_one, precision=precise)
            output = output + jnp.einsum('thd,hde->the', query_one, kv_state, precision=precise)
            new_state = kv_state + jnp.einsum('thd,the->hde', key_one, value_one, precision=precise)
            return (new_state, output)
        zero_state = jnp.zeros((H, DH, DH), jnp.float32)
        final_state, outputs = lax.scan(block_step, zero_state, (query_blk, key_blk, value_blk))
        return attn_scale * outputs.reshape(TOKENS, H, DH)
    query_f = queries.astype(jnp.float32).reshape(TOKENS, H, DH)
    key_f = keys.astype(jnp.float32).reshape(TOKENS, H, DH)
    value_f = values.astype(jnp.float32).reshape(TOKENS, H, DH)
    attn_f, pullback = jax.vjp(attend, query_f, key_f, value_f)
    attn = attn_f.reshape(TOKENS, H * DH).astype(jnp.bfloat16)
    group_width = HEADS_DEV * DH
    predicted = jnp.zeros((TOKENS, DM), jnp.float32)
    for group_idx in range(N_HEAD):
        lower = group_idx * group_width
        partial_value = jnp.dot(attn[:, lower:lower + group_width], out_weight[lower:lower + group_width], preferred_element_type=jnp.float32)
        rounded = lax.optimization_barrier(partial_value.astype(jnp.bfloat16))
        predicted = predicted + rounded.astype(jnp.float32)
    valid_total = jnp.sum(valid).astype(jnp.float32)
    residual_err = predicted - teacher.astype(jnp.float32)
    error_grad = (valid.astype(jnp.float32)[:, None] * residual_err * (TOKENS / valid_total)).astype(jnp.bfloat16)
    attn_grad = jnp.dot(error_grad, out_weight.T, preferred_element_type=jnp.float32)
    q_grad, k_grad, v_grad = pullback(attn_grad.reshape(TOKENS, H, DH))
    return (q_grad.reshape(TOKENS, H * DH), k_grad.reshape(TOKENS, H * DH), v_grad.reshape(TOKENS, H * DH))
```

```python
import functools
import math

import jax
import jax.numpy as jnp
from jax import lax
from jax.experimental import pallas as pl
from jax.experimental.pallas import tpu as pltpu
from jax.sharding import PartitionSpec as P

DH = 128
MESH = pl.DeviceIdType.MESH
F32 = jnp.float32
BF16 = jnp.bfloat16
NT = (((1,), (1,)), ((), ()))
TN = (((0,), (0,)), ((), ()))
NN = (((1,), (0,)), ((), ()))


def dot(a, b, dims):
    return lax.dot_general(a, b, dims, preferred_element_type=F32)


def lanes(start, size):
    return pl.ds(pl.multiple_of(start, 128), size)


def transfer(scale, heads, n_ctx, n_x, tokens,
             q_hbm, k_hbm, v_hbm, teacher_hbm, w_hbm, valid_ref,
             g_out, prefix_out, suffix_out,
             q, k, v, teacher, w, intra, attn, tp, trecv, relay_p, relay_m, fin_p, fin_m,
             gath, acc, g, loc, got, pre, state, loc2, got2, pre2, state2, cnt, cnts,
             in_sem, out_sem, a_s, a_r, b_s, b_r, c_s, c_r, d_s, d_r, n_s, n_r,
             t_s, t_r, x_s, x_r, gp_s, gp_r, gx_s, gx_r):
    rows = q.shape[0]
    half = rows // 2
    wide = w.shape[1] // n_x
    part = wide // 2
    me_c = lax.axis_index("ctx")
    me_h = lax.axis_index("head")
    x, core = me_h // 2, me_h % 2
    right = ((x + 1) % n_x) * 2 + core
    left = ((x + n_x - 1) % n_x) * 2 + core
    other = x * 2 + 1 - core
    pr = heads * DH // n_ctx

    barrier = pltpu.get_barrier_semaphore()
    for d in range(1, n_ctx):
        pl.semaphore_signal(barrier, inc=1, device_id=((me_c + d) % n_ctx, me_h), device_id_type=MESH)
    for h in (other, right, left):
        pl.semaphore_signal(barrier, inc=1, device_id=(me_c, h), device_id_type=MESH)

    loads = [
        pltpu.make_async_copy(src, dst, in_sem.at[i])
        for i, (src, dst) in enumerate(((k_hbm, k), (v_hbm, v), (q_hbm, q), (w_hbm, w), (teacher_hbm, teacher)))
    ]
    for one in loads:
        one.start()

    def peers(sending, src, dst, ssem, rsem, piece):
        out = []
        for d in range(1, n_ctx):
            peer = (me_c + d) % n_ctx if sending else (me_c + n_ctx - d) % n_ctx
            place = me_c if sending else peer
            out.append(pltpu.make_async_remote_copy(
                src_ref=src.at[pl.ds(pl.multiple_of(peer * piece, piece), piece)] if src is not cnt else src,
                dst_ref=dst.at[pl.ds(pl.multiple_of(place * piece, piece), piece)],
                send_sem=ssem.at[d],
                recv_sem=rsem.at[place],
                device_id=(peer, me_h),
                device_id_type=MESH,
            ))
        return out

    def mine(piece):
        return pl.ds(pl.multiple_of(me_c * piece, piece), piece)

    def scan(got_ref, pre_ref, backward):
        total = jnp.zeros((pr, DH), F32)
        order = range(n_ctx - 1, -1, -1) if backward else range(n_ctx)
        for j in order:
            block = slice(j * pr, (j + 1) * pr)
            pre_ref[block, :] = total.astype(BF16)
            total = total + got_ref[block, :].astype(F32)

    def start(copies):
        for one in copies:
            one.start()

    def finish_recv(copies):
        for one in copies:
            one.wait_recv()

    def finish_send(copies):
        for one in copies:
            one.wait_send()

    loads[0].wait()
    loads[1].wait()

    @pl.loop(0, heads)
    def _(h):
        cols = lanes(h * DH, DH)
        loc[pl.ds(pl.multiple_of(h * DH, DH), DH), :] = dot(k[:, cols], v[:, cols], TN).astype(BF16)

    cnt[...] = jnp.zeros_like(cnt) + jnp.sum(valid_ref[...])
    pl.semaphore_wait(barrier, n_ctx - 1 + 3)

    a_send = peers(True, loc, got, a_s, a_r, pr)
    n_send = peers(True, cnt, cnts, n_s, n_r, 8)
    start(a_send)
    start(n_send)
    got[mine(pr), :] = loc[mine(pr), :]
    cnts[mine(8), :] = cnt[...]

    loads[2].wait()
    row = lax.broadcasted_iota(jnp.int32, (half, half), 0)
    col = lax.broadcasted_iota(jnp.int32, (half, half), 1)
    lower = row >= col

    @pl.loop(0, heads)
    def _(h):
        cols = lanes(h * DH, DH)
        k0, k1 = k[0:half, cols], k[half:rows, cols]
        v0, v1 = v[0:half, cols], v[half:rows, cols]
        q0, q1 = q[0:half, cols], q[half:rows, cols]
        s0 = jnp.where(lower, dot(q0, k0, NT), 0.0).astype(BF16)
        intra[0:half, cols] = dot(s0, v0, NN)
        s10 = dot(q1, k0, NT).astype(BF16)
        s11 = jnp.where(lower, dot(q1, k1, NT), 0.0).astype(BF16)
        intra[half:rows, cols] = dot(s10, v0, NN) + dot(s11, v1, NN)

    finish_recv(peers(False, loc, got, a_s, a_r, pr))
    scan(got, pre, False)
    b_send = peers(True, pre, state, b_s, b_r, pr)
    start(b_send)
    state[mine(pr), :] = pre[mine(pr), :]
    finish_send(a_send)
    finish_send(n_send)
    finish_recv(peers(False, cnt, cnts, n_s, n_r, 8))
    count = cnts[0:8, :]
    for j in range(1, n_ctx):
        count = count + cnts[j * 8 : j * 8 + 8, :]
    cnt[...] = tokens / count
    loads[3].wait()
    loads[4].wait()
    finish_recv(peers(False, pre, state, b_s, b_r, pr))

    @pl.loop(0, heads)
    def _(h):
        cols = lanes(h * DH, DH)
        carried = dot(q[:, cols], state[pl.ds(pl.multiple_of(h * DH, DH), DH), :], NN)
        attn[:, cols] = (scale * (intra[:, cols] + carried)).astype(BF16)

    def remote(src, dst, ssem, rsem, device):
        return pltpu.make_async_remote_copy(
            src_ref=src, dst_ref=dst, send_sem=ssem, recv_sem=rsem,
            device_id=(me_c, device), device_id_type=MESH)

    own = lanes(core * part, part)
    theirs = lanes((1 - core) * part, part)
    first, second = pl.ds(0, half), pl.ds(half, half)
    step_rows = 64

    t_copies, x_copies = [], []
    targets = [(x + 2) % n_x, (x + 1) % n_x, (x + 3) % n_x, x]

    def terms(i):
        base = targets[i] * wide

        @pl.loop(0, wide // 256)
        def _(n):
            tp[i, :, lanes(n * 256, 256)] = dot(attn[...], w[:, lanes(base + n * 256, 256)], NN).astype(BF16)

        copy = remote(tp.at[i, :, theirs], trecv.at[i], t_s.at[i], t_r.at[i], other)
        copy.start()
        t_copies.append(copy)

    def add_chip(i):
        t_copies[i].wait_recv()

        @pl.loop(0, rows // step_rows)
        def _(r):
            at = pl.ds(pl.multiple_of(r * step_rows, step_rows), step_rows)
            tp[i, at, own] = (tp[i, at, own].astype(F32) + trecv[i, at, :].astype(F32)).astype(BF16)

    def add_relay(i, rel, base):
        @pl.loop(0, half // step_rows)
        def _(r):
            off = pl.multiple_of(r * step_rows, step_rows)
            at = pl.ds(base + off, step_rows)
            tp[i, at, own] = (tp[i, at, own].astype(F32) + rel[pl.ds(off, step_rows), :].astype(F32)).astype(BF16)

    def send_x(n, src, dst, device):
        copy = remote(src, dst, x_s.at[n], x_r.at[n], device)
        copy.start()
        x_copies.append(copy)

    terms(0)
    terms(1)
    add_chip(0)
    send_x(0, tp.at[0, first, own], relay_p, right)
    send_x(1, tp.at[0, second, own], relay_m, left)
    terms(2)
    add_chip(1)
    send_x(2, tp.at[1, second, own], fin_p.at[second], right)
    terms(3)
    add_chip(2)
    send_x(3, tp.at[2, first, own], fin_m.at[first], left)
    x_copies[0].wait_recv()
    add_relay(1, relay_p, 0)
    send_x(4, tp.at[1, first, own], fin_p.at[first], right)
    x_copies[1].wait_recv()
    add_relay(2, relay_m, half)
    send_x(5, tp.at[2, second, own], fin_m.at[second], left)
    t_copies[3].wait_recv()

    def error(base):
        @pl.loop(0, half // step_rows)
        def _(r):
            at = pl.ds(pl.multiple_of(base + r * step_rows, step_rows), step_rows)
            pred = tp[3, at, own].astype(F32) + trecv[3, at, :].astype(F32)
            pred = pred + fin_p[at, :].astype(F32) + fin_m[at, :].astype(F32)
            miss = pred - teacher[at, :].astype(F32)
            gath[x, at, own] = (valid_ref[at, :] * miss * cnt[0:1, 0:1]).astype(BF16)

    gp_copies, gx_copies = {}, {}

    def to_other(n, block, at):
        ref = gath.at[block, at, own]
        copy = remote(ref, ref, gp_s.at[n], gp_r.at[n], other)
        copy.start()
        gp_copies[n] = copy

    def from_other(n, block, at):
        ref = gath.at[block, at, theirs]
        remote(ref, ref, gp_s.at[n], gp_r.at[n], other).wait_recv()

    def to_x(n, block, at, device):
        ref = gath.at[block, at, own]
        copy = remote(ref, ref, gx_s.at[n], gx_r.at[n], device)
        copy.start()
        gx_copies[n] = copy

    def from_x(n, block, at, device):
        ref = gath.at[block, at, own]
        remote(ref, ref, gx_s.at[n], gx_r.at[n], device).wait_recv()

    far, near_l, near_r = (x + 2) % n_x, (x + 3) % n_x, (x + 1) % n_x
    x_copies[3].wait_recv()
    x_copies[4].wait_recv()
    error(0)
    to_x(0, x, first, right)
    to_other(0, x, first)
    x_copies[2].wait_recv()
    x_copies[5].wait_recv()
    error(half)
    to_x(1, x, second, left)
    to_x(2, x, second, right)
    to_x(3, x, first, left)
    to_other(1, x, second)

    def contract(block, base, fresh=False):
        @pl.loop(0, heads * DH // 256)
        def _(n):
            at = pl.ds(base, half)
            cols = lanes(n * 256, 256)
            new = dot(
                gath[block, at, :],
                w[pl.ds(pl.multiple_of(n * 256, 256), 256), lanes(block * wide, wide)],
                NT,
            )
            acc[at, cols] = new if fresh else acc[at, cols] + new

    from_other(0, x, first)
    contract(x, 0, True)
    from_x(0, near_l, first, left)
    to_x(4, near_l, first, right)
    to_other(2, near_l, first)
    from_x(1, near_r, second, right)
    to_x(5, near_r, second, left)
    to_other(3, near_r, second)
    from_other(1, x, second)
    contract(x, half, True)
    from_other(2, near_l, first)
    contract(near_l, 0)
    from_other(3, near_r, second)
    contract(near_r, half)
    from_x(2, near_l, second, left)
    to_other(4, near_l, second)
    from_x(3, near_r, first, right)
    to_other(5, near_r, first)
    from_other(4, near_l, second)
    contract(near_l, half)
    from_other(5, near_r, first)
    contract(near_r, 0)
    from_x(4, far, first, left)
    to_other(6, far, first)
    from_x(5, far, second, right)
    to_other(7, far, second)
    from_other(6, far, first)
    contract(far, 0)
    from_other(7, far, second)
    contract(far, half)

    @pl.loop(0, heads)
    def _(h):
        cols = lanes(h * DH, DH)
        g_h = acc[:, cols].astype(BF16)
        g[:, cols] = g_h
        loc2[pl.ds(pl.multiple_of(h * DH, DH), DH), :] = dot(q[:, cols], g_h, TN).astype(BF16)

    c_send = peers(True, loc2, got2, c_s, c_r, pr)
    start(c_send)
    got2[mine(pr), :] = loc2[mine(pr), :]
    outs = [
        pltpu.make_async_copy(g, g_out, out_sem.at[0]),
        pltpu.make_async_copy(state, prefix_out, out_sem.at[1]),
    ]
    start(outs)
    finish_send(b_send)
    finish_send(t_copies)
    finish_send(x_copies)
    finish_send(gp_copies.values())
    finish_send(gx_copies.values())
    finish_recv(peers(False, loc2, got2, c_s, c_r, pr))
    scan(got2, pre2, True)
    d_send = peers(True, pre2, state2, d_s, d_r, pr)
    start(d_send)
    state2[mine(pr), :] = pre2[mine(pr), :]
    finish_send(c_send)
    finish_recv(peers(False, pre2, state2, d_s, d_r, pr))
    last = pltpu.make_async_copy(state2, suffix_out, out_sem.at[2])
    last.start()
    finish_send(d_send)
    for one in outs:
        one.wait()
    last.wait()


def gradients(scale, per, q_ref, k_ref, v_ref, g_ref, p_ref, r_ref, dq_ref, dk_ref, dv_ref):
    rows = q_ref.shape[0]
    half = rows // 2
    row = lax.broadcasted_iota(jnp.int32, (half, half), 0)
    col = lax.broadcasted_iota(jnp.int32, (half, half), 1)
    lower = row >= col
    upper = row <= col
    for h in range(per):
        cols = slice(h * DH, (h + 1) * DH)
        q0, q1 = q_ref[0:half, cols], q_ref[half:rows, cols]
        k0, k1 = k_ref[0:half, cols], k_ref[half:rows, cols]
        v0, v1 = v_ref[0:half, cols], v_ref[half:rows, cols]
        g0, g1 = g_ref[0:half, cols], g_ref[half:rows, cols]
        p, r = p_ref[cols, :], r_ref[cols, :]

        def tri(a, b, mask):
            return jnp.where(mask, dot(a, b, NT), 0.0).astype(BF16)

        def full(a, b):
            return dot(a, b, NT).astype(BF16)

        dq_ref[0:half, cols] = scale * (dot(tri(g0, v0, lower), k0, NN) + dot(g0, p, NT))
        dq_ref[half:rows, cols] = scale * (
            dot(full(g1, v0), k0, NN) + dot(tri(g1, v1, lower), k1, NN) + dot(g1, p, NT)
        )
        dk_ref[0:half, cols] = scale * (
            dot(tri(v0, g0, upper), q0, NN) + dot(full(v0, g1), q1, NN) + dot(v0, r, NT)
        )
        dk_ref[half:rows, cols] = scale * (dot(tri(v1, g1, upper), q1, NN) + dot(v1, r, NT))
        dv_ref[0:half, cols] = scale * (
            dot(tri(k0, q0, upper), g0, NN) + dot(full(k0, q1), g1, NN) + dot(k0, r, NN)
        )
        dv_ref[half:rows, cols] = scale * (dot(tri(k1, q1, upper), g1, NN) + dot(k1, r, NN))


def on_device(queries, keys, values, teacher, out_weight, valid):
    rows, width = queries.shape
    heads = width // DH
    model = out_weight.shape[1]
    n_ctx = lax.axis_size("ctx")
    n_x = lax.axis_size("head") // 2
    half = rows // 2
    wide = model // n_x
    part = wide // 2
    tokens = float(rows * n_ctx)
    scale = 1.0 / math.sqrt(DH * rows * n_ctx)
    valid_col = valid.astype(F32).reshape(rows, 1)
    anywhere = pl.BlockSpec(memory_space=pl.ANY)
    vmem = pl.BlockSpec(memory_space=pltpu.VMEM)
    dma = pltpu.SemaphoreType.DMA
    st = lambda: pltpu.VMEM((heads * DH, DH), BF16)
    g, prefix, suffix = pl.pallas_call(
        functools.partial(transfer, scale, heads, n_ctx, n_x, tokens),
        name="transfer",
        out_shape=(
            jax.ShapeDtypeStruct((rows, width), BF16),
            jax.ShapeDtypeStruct((width, DH), BF16),
            jax.ShapeDtypeStruct((width, DH), BF16),
        ),
        in_specs=[anywhere] * 5 + [vmem],
        out_specs=(anywhere,) * 3,
        scratch_shapes=[
            pltpu.VMEM((rows, width), BF16),
            pltpu.VMEM((rows, width), BF16),
            pltpu.VMEM((rows, width), BF16),
            pltpu.VMEM((rows, part), BF16),
            pltpu.VMEM((width, model), BF16),
            pltpu.VMEM((rows, width), F32),
            pltpu.VMEM((rows, width), BF16),
            pltpu.VMEM((4, rows, wide), BF16),
            pltpu.VMEM((4, rows, part), BF16),
            pltpu.VMEM((half, part), BF16),
            pltpu.VMEM((half, part), BF16),
            pltpu.VMEM((rows, part), BF16),
            pltpu.VMEM((rows, part), BF16),
            pltpu.VMEM((n_x, rows, wide), BF16),
            pltpu.VMEM((rows, width), F32),
            pltpu.VMEM((rows, width), BF16),
            st(), st(), st(), st(), st(), st(), st(), st(),
            pltpu.VMEM((8, 128), F32),
            pltpu.VMEM((8 * n_ctx, 128), F32),
            dma((5,)), dma((3,)),
            dma((n_ctx,)), dma((n_ctx,)), dma((n_ctx,)), dma((n_ctx,)),
            dma((n_ctx,)), dma((n_ctx,)), dma((n_ctx,)), dma((n_ctx,)),
            dma((n_ctx,)), dma((n_ctx,)),
            dma((4,)), dma((4,)), dma((6,)), dma((6,)),
            dma((8,)), dma((8,)), dma((6,)), dma((6,)),
        ],
        compiler_params=pltpu.CompilerParams(
            collective_id=0, has_side_effects=True, vmem_limit_bytes=60 * 1024 * 1024
        ),
    )(queries, keys, values, teacher, out_weight, valid_col)

    per = 2
    block = pl.BlockSpec((rows, per * DH), lambda i: (0, i))
    square = pl.BlockSpec((per * DH, DH), lambda i: (i, 0))
    out = jax.ShapeDtypeStruct((rows, width), F32)
    return tuple(pl.pallas_call(
        functools.partial(gradients, scale, per),
        name="gradients",
        grid=(heads // per,),
        out_shape=(out, out, out),
        in_specs=[block] * 4 + [square] * 2,
        out_specs=(block,) * 3,
    )(queries, keys, values, g, prefix, suffix))


def solution(mesh):
    in_specs = (
        P("ctx", "head"),
        P("ctx", "head"),
        P("ctx", "head"),
        P("ctx", "head"),
        P("head", None),
        P("ctx"),
    )
    out_specs = (P("ctx", "head"), P("ctx", "head"), P("ctx", "head"))
    return jax.shard_map(
        on_device, mesh=mesh, in_specs=in_specs, out_specs=out_specs, check_vma=False
    )
```

```python
import functools
import math

import jax
import jax.numpy as jnp
from jax import lax
from jax.experimental import pallas as pl
from jax.experimental.pallas import tpu as pltpu
from jax.sharding import PartitionSpec as P

DH = 128
MESH = pl.DeviceIdType.MESH
F32 = jnp.float32
BF16 = jnp.bfloat16
NT = (((1,), (1,)), ((), ()))
TN = (((0,), (0,)), ((), ()))
NN = (((1,), (0,)), ((), ()))


def dot(a, b, dims):
    return lax.dot_general(a, b, dims, preferred_element_type=F32)


def lanes(start, size):
    return pl.ds(pl.multiple_of(start, 128), size)


def transfer(scale, heads, n_ctx, n_x, tokens,
             q_hbm, k_hbm, v_hbm, teacher_hbm, w_hbm, valid_ref,
             dq_out, dk_out, dv_out, suffix_out,
             q, k, v, teacher, w, intra, attn, tp, trecv, relay_p, relay_m, fin_p, fin_m,
             gath, acc, g, dk, dv, weight, loc, got, pre, state, loc2, got2, pre2, state2, cnt, cnts,
             in_sem, out_sem, a_s, a_r, b_s, b_r, c_s, c_r, d_s, d_r, n_s, n_r,
             t_s, t_r, x_s, x_r, gp_s, gp_r, gx_s, gx_r):
    dq = intra
    rows = q.shape[0]
    half = rows // 2
    quarter = rows // 4
    wide = w.shape[1] // n_x
    part = wide // 2
    me_c = lax.axis_index("ctx")
    me_h = lax.axis_index("head")
    x, core = me_h // 2, me_h % 2
    right = ((x + 1) % n_x) * 2 + core
    left = ((x + n_x - 1) % n_x) * 2 + core
    other = x * 2 + 1 - core
    pr = heads * DH // n_ctx

    barrier = pltpu.get_barrier_semaphore()
    for d in range(1, n_ctx):
        pl.semaphore_signal(barrier, inc=1, device_id=((me_c + d) % n_ctx, me_h), device_id_type=MESH)
    for h in (other, right, left):
        pl.semaphore_signal(barrier, inc=1, device_id=(me_c, h), device_id_type=MESH)

    loads = [
        pltpu.make_async_copy(src, dst, in_sem.at[i])
        for i, (src, dst) in enumerate(((k_hbm, k), (v_hbm, v), (q_hbm, q), (w_hbm, w), (teacher_hbm, teacher)))
    ]
    for one in loads[:3]:
        one.start()

    def peers(sending, src, dst, ssem, rsem, piece):
        out = []
        for d in range(1, n_ctx):
            peer = (me_c + d) % n_ctx if sending else (me_c + n_ctx - d) % n_ctx
            place = me_c if sending else peer
            out.append(pltpu.make_async_remote_copy(
                src_ref=src.at[pl.ds(pl.multiple_of(peer * piece, piece), piece)] if src is not cnt else src,
                dst_ref=dst.at[pl.ds(pl.multiple_of(place * piece, piece), piece)],
                send_sem=ssem.at[d],
                recv_sem=rsem.at[place],
                device_id=(peer, me_h),
                device_id_type=MESH,
            ))
        return out

    def mine(piece):
        return pl.ds(pl.multiple_of(me_c * piece, piece), piece)

    def head_rows(h):
        return pl.ds(pl.multiple_of(h * DH, DH), DH)

    def scan(got_ref, pre_ref, backward):
        total = jnp.zeros((pr, DH), F32)
        order = range(n_ctx - 1, -1, -1) if backward else range(n_ctx)
        for j in order:
            block = slice(j * pr, (j + 1) * pr)
            pre_ref[block, :] = total.astype(BF16)
            total = total + got_ref[block, :].astype(F32)

    def start(copies):
        for one in copies:
            one.start()

    def finish_recv(copies):
        for one in copies:
            one.wait_recv()

    def finish_send(copies):
        for one in copies:
            one.wait_send()

    loads[0].wait()
    loads[1].wait()

    @pl.loop(0, heads)
    def _(h):
        cols = lanes(h * DH, DH)
        loc[head_rows(h), :] = dot(k[:, cols], v[:, cols], TN).astype(BF16)

    loads[3].start()
    loads[4].start()
    flags = valid_ref[...].astype(F32)
    cnt[...] = jnp.zeros_like(cnt) + jnp.sum(flags)
    pl.semaphore_wait(barrier, n_ctx - 1 + 3)

    a_send = peers(True, loc, got, a_s, a_r, pr)
    n_send = peers(True, cnt, cnts, n_s, n_r, 8)
    start(a_send)
    start(n_send)
    got[mine(pr), :] = loc[mine(pr), :]
    cnts[mine(8), :] = cnt[...]

    loads[2].wait()
    row = lax.broadcasted_iota(jnp.int32, (half, half), 0)
    col = lax.broadcasted_iota(jnp.int32, (half, half), 1)
    lower = row >= col
    upper = row <= col

    def both(ref, cols):
        return ref[0:half, cols], ref[half:rows, cols]

    def full(a, b):
        return dot(a, b, NT).astype(BF16)

    def tri(a, b, mask):
        return jnp.where(mask, dot(a, b, NT), 0.0).astype(BF16)

    @pl.loop(0, heads)
    def _(h):
        cols = lanes(h * DH, DH)
        (k0, k1), (v0, v1), (q0, q1) = both(k, cols), both(v, cols), both(q, cols)
        intra[0:half, cols] = dot(tri(q0, k0, lower), v0, NN)
        intra[half:rows, cols] = dot(full(q1, k0), v0, NN) + dot(tri(q1, k1, lower), v1, NN)

    finish_recv(peers(False, loc, got, a_s, a_r, pr))
    scan(got, pre, False)
    b_send = peers(True, pre, state, b_s, b_r, pr)
    start(b_send)
    state[mine(pr), :] = pre[mine(pr), :]
    finish_send(a_send)
    finish_send(n_send)
    finish_recv(peers(False, cnt, cnts, n_s, n_r, 8))
    count = cnts[0:8, :]
    for j in range(1, n_ctx):
        count = count + cnts[j * 8 : j * 8 + 8, :]
    factor = (tokens / count)[0:1, :]
    diagonal = row[0:DH, 0:DH] == col[0:DH, 0:DH]
    for j in range(rows // DH):
        column = jnp.sum(jnp.where(diagonal, flags[j : j + 1, :], 0.0), axis=1, keepdims=True)
        weight[j * DH : (j + 1) * DH, :] = column * factor
    loads[3].wait()
    loads[4].wait()
    finish_recv(peers(False, pre, state, b_s, b_r, pr))

    def attend(base):
        at = pl.ds(base, half)

        @pl.loop(0, heads)
        def _(h):
            cols = lanes(h * DH, DH)
            carried = dot(q[at, cols], state[head_rows(h), :], NN)
            attn[at, cols] = (scale * (intra[at, cols] + carried)).astype(BF16)

    def remote(src, dst, ssem, rsem, device):
        return pltpu.make_async_remote_copy(
            src_ref=src, dst_ref=dst, send_sem=ssem, recv_sem=rsem,
            device_id=(me_c, device), device_id_type=MESH)

    own = lanes(core * part, part)
    theirs = lanes((1 - core) * part, part)
    step_rows = 64
    sent = []

    def send(src, dst, ssem, rsem, n, device):
        copy = remote(src, dst, ssem.at[n], rsem.at[n], device)
        copy.start()
        sent.append(copy)
        return copy

    def quarters(c):
        return pl.ds(2 * c * quarter, quarter), pl.ds((2 * c + 1) * quarter, quarter)

    near_r, near_l, far = (x + 1) % n_x, (x + n_x - 1) % n_x, (x + 2) % n_x
    targets = [far, near_r, near_l, x]
    t_copies, x_copies = {}, {}

    def terms(i, c):
        at = pl.ds(c * half, half)
        base = targets[i] * wide

        @pl.loop(0, wide // 256)
        def _(n):
            tp[i, at, lanes(n * 256, 256)] = dot(attn[at, :], w[:, lanes(base + n * 256, 256)], NN).astype(BF16)

        t_copies[i, c] = send(tp.at[i, at, theirs], trecv.at[i, at, :], t_s, t_r, 4 * c + i, other)

    def add_chip(i, c):
        t_copies[i, c].wait_recv()

        @pl.loop(0, half // step_rows)
        def _(r):
            at = pl.ds(pl.multiple_of(c * half + r * step_rows, step_rows), step_rows)
            tp[i, at, own] = (tp[i, at, own].astype(F32) + trecv[i, at, :].astype(F32)).astype(BF16)

    def add_relay(i, rel, c, base):
        @pl.loop(0, quarter // step_rows)
        def _(r):
            off = pl.multiple_of(r * step_rows, step_rows)
            at = pl.ds(base + off, step_rows)
            tp[i, at, own] = (tp[i, at, own].astype(F32) + rel[c, pl.ds(off, step_rows), :].astype(F32)).astype(BF16)

    def send_x(n, c, src, dst, device):
        x_copies[n, c] = send(src, dst, x_s, x_r, 6 * c + n, device)

    def far_out(c):
        qa, qb = quarters(c)
        add_chip(0, c)
        send_x(0, c, tp.at[0, qa, own], relay_p.at[c], right)
        send_x(1, c, tp.at[0, qb, own], relay_m.at[c], left)

    def right_out(c):
        qa, qb = quarters(c)
        add_chip(1, c)
        send_x(2, c, tp.at[1, qb, own], fin_p.at[qb], right)

    def left_out(c):
        qa, qb = quarters(c)
        add_chip(2, c)
        send_x(3, c, tp.at[2, qa, own], fin_m.at[qa], left)

    def relayed(c):
        qa, qb = quarters(c)
        x_copies[0, c].wait_recv()
        add_relay(1, relay_p, c, 2 * c * quarter)
        send_x(4, c, tp.at[1, qa, own], fin_p.at[qa], right)
        x_copies[1, c].wait_recv()
        add_relay(2, relay_m, c, (2 * c + 1) * quarter)
        send_x(5, c, tp.at[2, qb, own], fin_m.at[qb], left)

    def to_other(n, c, block, at):
        ref = gath.at[block, at, own]
        send(ref, ref, gp_s, gp_r, 7 * c + n, other)

    def from_other(n, c, block, at):
        ref = gath.at[block, at, theirs]
        remote(ref, ref, gp_s.at[7 * c + n], gp_r.at[7 * c + n], other).wait_recv()

    def to_x(n, c, block, at, device):
        ref = gath.at[block, at, own]
        send(ref, ref, gx_s, gx_r, 6 * c + n, device)

    def from_x(n, c, block, at, device):
        ref = gath.at[block, at, own]
        remote(ref, ref, gx_s.at[6 * c + n], gx_r.at[6 * c + n], device).wait_recv()

    def error(c):
        t_copies[3, c].wait_recv()
        for n in (2, 3, 4, 5):
            x_copies[n, c].wait_recv()

        @pl.loop(0, half // step_rows)
        def _(r):
            at = pl.ds(pl.multiple_of(c * half + r * step_rows, step_rows), step_rows)
            pred = tp[3, at, own].astype(F32) + trecv[3, at, :].astype(F32)
            pred = pred + fin_p[at, :].astype(F32) + fin_m[at, :].astype(F32)
            miss = pred - teacher[at, :].astype(F32)
            gath[x, at, own] = (miss * jnp.concatenate([weight[at, :]] * (part // DH), axis=1)).astype(BF16)

        qa, qb = quarters(c)
        to_x(0, c, x, qa, right)
        to_x(1, c, x, qb, left)
        to_x(2, c, x, qb, right)
        to_x(3, c, x, qa, left)
        to_other(0, c, x, pl.ds(c * half, half))

    def near_first(c):
        qa, qb = quarters(c)
        from_x(0, c, near_l, qa, left)
        to_x(4, c, near_l, qa, right)
        to_other(1, c, near_l, qa)
        from_x(1, c, near_r, qb, right)
        to_x(5, c, near_r, qb, left)
        to_other(2, c, near_r, qb)

    def near_second(c):
        qa, qb = quarters(c)
        from_x(2, c, near_l, qb, left)
        to_other(3, c, near_l, qb)
        from_x(3, c, near_r, qa, right)
        to_other(4, c, near_r, qa)

    def far_in(c):
        qa, qb = quarters(c)
        from_x(4, c, far, qa, left)
        to_other(5, c, far, qa)
        from_x(5, c, far, qb, right)
        to_other(6, c, far, qb)

    def contract(block, c, lo=0, size=wide, fresh=False):
        at = pl.ds(c * half, half)

        @pl.loop(0, heads * DH // 256)
        def _(n):
            cols = lanes(n * 256, 256)
            new = dot(
                gath[block, at, lanes(lo, size)],
                w[lanes(n * 256, 256), lanes(block * wide + lo, size)],
                NT,
            )
            acc[at, cols] = new if fresh else acc[at, cols] + new

    def contract_own(c):
        from_other(0, c, x, pl.ds(c * half, half))
        contract(x, c, fresh=True)

    def contract_near(c):
        qa, qb = quarters(c)
        from_other(1, c, near_l, qa)
        from_other(3, c, near_l, qb)
        contract(near_l, c)
        from_other(2, c, near_r, qb)
        from_other(4, c, near_r, qa)
        contract(near_r, c)

    def contract_far(c):
        qa, qb = quarters(c)
        contract(far, c, core * part, part)
        from_other(5, c, far, qa)
        from_other(6, c, far, qb)
        contract(far, c, (1 - core) * part, part)

    attend(0)
    terms(0, 0)
    terms(1, 0)
    far_out(0)
    terms(2, 0)
    right_out(0)
    terms(3, 0)
    left_out(0)
    attend(half)
    terms(0, 1)
    relayed(0)
    terms(1, 1)
    far_out(1)
    terms(2, 1)
    right_out(1)
    terms(3, 1)
    left_out(1)
    error(0)
    relayed(1)
    contract_own(0)
    near_first(0)
    near_second(0)
    contract_near(0)
    error(1)
    contract_own(1)
    far_in(0)
    contract_far(0)

    @pl.loop(0, heads)
    def _(h):
        cols = lanes(h * DH, DH)
        g_h = acc[0:half, cols].astype(BF16)
        g[0:half, cols] = g_h
        acc[0:DH, cols] = dot(q[0:half, cols], g_h, TN)

    near_first(1)

    @pl.loop(0, heads)
    def _(h):
        cols = lanes(h * DH, DH)
        k0, v0, q0, g0 = k[0:half, cols], v[0:half, cols], q[0:half, cols], g[0:half, cols]
        dq[0:half, cols] = dot(tri(g0, v0, lower), k0, NN) + dot(g0, state[head_rows(h), :], NT)
        dk[0:half, cols] = dot(tri(v0, g0, upper), q0, NN)
        dv[0:half, cols] = dot(tri(k0, q0, upper), g0, NN)

    near_second(1)
    contract_near(1)
    far_in(1)
    contract_far(1)

    @pl.loop(0, heads)
    def _(h):
        cols = lanes(h * DH, DH)
        g_h = acc[half:rows, cols].astype(BF16)
        g[half:rows, cols] = g_h
        loc2[head_rows(h), :] = (acc[0:DH, cols] + dot(q[half:rows, cols], g_h, TN)).astype(BF16)

    c_send = peers(True, loc2, got2, c_s, c_r, pr)
    start(c_send)
    got2[mine(pr), :] = loc2[mine(pr), :]

    outs = []

    def second_half(lo, hi):
        @pl.loop(lo, hi)
        def _(h):
            cols = lanes(h * DH, DH)
            (k0, k1), (v0, v1), (q0, q1) = both(k, cols), both(v, cols), both(q, cols)
            g1 = g[half:rows, cols]
            dq[half:rows, cols] = (
                dot(full(g1, v0), k0, NN) + dot(tri(g1, v1, lower), k1, NN)
                + dot(g1, state[head_rows(h), :], NT)
            )
            dk[0:half, cols] += dot(full(v0, g1), q1, NN)
            dk[half:rows, cols] = dot(tri(v1, g1, upper), q1, NN)
            dv[0:half, cols] += dot(full(k0, q1), g1, NN)
            dv[half:rows, cols] = dot(tri(k1, q1, upper), g1, NN)

        cols = pl.ds(lo * DH, (hi - lo) * DH)
        for src, dst in ((dq, dq_out), (dk, dk_out), (dv, dv_out)):
            copy = pltpu.make_async_copy(src.at[:, cols], dst.at[:, cols], out_sem.at[len(outs)])
            copy.start()
            outs.append(copy)

    second_half(0, heads // 2)
    finish_recv(peers(False, loc2, got2, c_s, c_r, pr))
    scan(got2, pre2, True)
    d_send = peers(True, pre2, state2, d_s, d_r, pr)
    start(d_send)
    state2[mine(pr), :] = pre2[mine(pr), :]
    second_half(heads // 2, heads)
    finish_send(b_send)
    finish_send(sent)
    finish_send(c_send)
    finish_recv(peers(False, pre2, state2, d_s, d_r, pr))
    last = pltpu.make_async_copy(state2, suffix_out, out_sem.at[6])
    last.start()
    finish_send(d_send)
    for one in outs:
        one.wait()
    last.wait()


def gradients(scale, per, k_ref, v_ref, pq_ref, pk_ref, pv_ref, r_ref, dq_ref, dk_ref, dv_ref):
    for h in range(per):
        cols = slice(h * DH, (h + 1) * DH)
        r = r_ref[cols, :]
        dq_ref[:, cols] = scale * pq_ref[:, cols]
        dk_ref[:, cols] = scale * (pk_ref[:, cols] + dot(v_ref[:, cols], r, NT))
        dv_ref[:, cols] = scale * (pv_ref[:, cols] + dot(k_ref[:, cols], r, NN))


def on_device(queries, keys, values, teacher, out_weight, valid):
    rows, width = queries.shape
    heads = width // DH
    model = out_weight.shape[1]
    n_ctx = lax.axis_size("ctx")
    n_x = lax.axis_size("head") // 2
    half = rows // 2
    wide = model // n_x
    part = wide // 2
    tokens = float(rows * n_ctx)
    scale = 1.0 / math.sqrt(DH * rows * n_ctx)
    valid_rows = valid.reshape(rows // DH, DH)
    anywhere = pl.BlockSpec(memory_space=pl.ANY)
    vmem = pl.BlockSpec(memory_space=pltpu.VMEM)
    dma = pltpu.SemaphoreType.DMA
    st = lambda: pltpu.VMEM((heads * DH, DH), BF16)
    whole = jax.ShapeDtypeStruct((rows, width), F32)
    dq, dk, dv, suffix = pl.pallas_call(
        functools.partial(transfer, scale, heads, n_ctx, n_x, tokens),
        name="transfer",
        out_shape=(whole, whole, whole, jax.ShapeDtypeStruct((width, DH), BF16)),
        in_specs=[anywhere] * 5 + [vmem],
        out_specs=(anywhere,) * 4,
        scratch_shapes=[
            pltpu.VMEM((rows, width), BF16),
            pltpu.VMEM((rows, width), BF16),
            pltpu.VMEM((rows, width), BF16),
            pltpu.VMEM((rows, part), BF16),
            pltpu.VMEM((width, model), BF16),
            pltpu.VMEM((rows, width), F32),
            pltpu.VMEM((rows, width), BF16),
            pltpu.VMEM((4, rows, wide), BF16),
            pltpu.VMEM((4, rows, part), BF16),
            pltpu.VMEM((2, half // 2, part), BF16),
            pltpu.VMEM((2, half // 2, part), BF16),
            pltpu.VMEM((rows, part), BF16),
            pltpu.VMEM((rows, part), BF16),
            pltpu.VMEM((n_x, rows, wide), BF16),
            pltpu.VMEM((rows, width), F32),
            pltpu.VMEM((rows, width), BF16),
            pltpu.VMEM((rows, width), F32),
            pltpu.VMEM((rows, width), F32),
            pltpu.VMEM((rows, DH), F32),
            st(), st(), st(), st(), st(), st(), st(), st(),
            pltpu.VMEM((8, 128), F32),
            pltpu.VMEM((8 * n_ctx, 128), F32),
            dma((5,)), dma((7,)),
            dma((n_ctx,)), dma((n_ctx,)), dma((n_ctx,)), dma((n_ctx,)),
            dma((n_ctx,)), dma((n_ctx,)), dma((n_ctx,)), dma((n_ctx,)),
            dma((n_ctx,)), dma((n_ctx,)),
            dma((8,)), dma((8,)), dma((12,)), dma((12,)),
            dma((14,)), dma((14,)), dma((12,)), dma((12,)),
        ],
        compiler_params=pltpu.CompilerParams(
            collective_id=0, has_side_effects=True, vmem_limit_bytes=60 * 1024 * 1024
        ),
    )(queries, keys, values, teacher, out_weight, valid_rows)

    per = 2
    block = pl.BlockSpec((rows, per * DH), lambda i: (0, i))
    square = pl.BlockSpec((per * DH, DH), lambda i: (i, 0))
    return tuple(pl.pallas_call(
        functools.partial(gradients, scale, per),
        name="gradients",
        grid=(heads // per,),
        out_shape=(whole, whole, whole),
        in_specs=[block] * 5 + [square],
        out_specs=(block,) * 3,
    )(keys, values, dq, dk, dv, suffix))


def solution(mesh):
    in_specs = (
        P("ctx", "head"),
        P("ctx", "head"),
        P("ctx", "head"),
        P("ctx", "head"),
        P("head", None),
        P("ctx"),
    )
    out_specs = (P("ctx", "head"), P("ctx", "head"), P("ctx", "head"))
    return jax.shard_map(
        on_device, mesh=mesh, in_specs=in_specs, out_specs=out_specs, check_vma=False
    )
```

```python
import functools
import math

import jax
import jax.numpy as jnp
from jax import lax
from jax.experimental import pallas as pl
from jax.experimental.pallas import tpu as pltpu
from jax.sharding import PartitionSpec as P

DH = 128
UT = True
UC = True
UG = 2
MESH = pl.DeviceIdType.MESH
F32 = jnp.float32
BF16 = jnp.bfloat16
NT = (((1,), (1,)), ((), ()))
TN = (((0,), (0,)), ((), ()))
NN = (((1,), (0,)), ((), ()))


def dot(a, b, dims):
    return lax.dot_general(a, b, dims, preferred_element_type=F32)


def lanes(start, size):
    return pl.ds(pl.multiple_of(start, 128), size)


def transfer(scale, heads, n_ctx, n_x, tokens,
             q_hbm, k_hbm, v_hbm, teacher_hbm, w_hbm, valid_ref,
             dq_out, dk_out, dv_out, suffix_out,
             q, k, v, teacher, w, intra, attn, tp, trecv, relay_p, relay_m, fin_p, fin_m,
             gath, acc, g, dq, dk, dv, weight, loc, got, pre, state, loc2, got2, pre2, state2, cnt, cnts,
             in_sem, out_sem, a_s, a_r, b_s, b_r, c_s, c_r, d_s, d_r, n_s, n_r,
             t_s, t_r, x_s, x_r, gp_s, gp_r, gx_s, gx_r):
    rows = q.shape[0]
    half = rows // 2
    quarter = rows // 4
    wide = w.shape[1] // n_x
    part = wide // 2
    me_c = lax.axis_index("ctx")
    me_h = lax.axis_index("head")
    x, core = me_h // 2, me_h % 2
    right = ((x + 1) % n_x) * 2 + core
    left = ((x + n_x - 1) % n_x) * 2 + core
    other = x * 2 + 1 - core
    pr = heads * DH // n_ctx

    barrier = pltpu.get_barrier_semaphore()
    for d in range(1, n_ctx):
        pl.semaphore_signal(barrier, inc=1, device_id=((me_c + d) % n_ctx, me_h), device_id_type=MESH)
    for h in (other, right, left):
        pl.semaphore_signal(barrier, inc=1, device_id=(me_c, h), device_id_type=MESH)

    loads = [
        pltpu.make_async_copy(src, dst, in_sem.at[i])
        for i, (src, dst) in enumerate(((k_hbm, k), (v_hbm, v), (q_hbm, q), (w_hbm, w), (teacher_hbm, teacher)))
    ]
    for one in loads[:3]:
        one.start()

    def peers(sending, src, dst, ssem, rsem, piece):
        out = []
        for d in range(1, n_ctx):
            peer = (me_c + d) % n_ctx if sending else (me_c + n_ctx - d) % n_ctx
            place = me_c if sending else peer
            out.append(pltpu.make_async_remote_copy(
                src_ref=src.at[pl.ds(pl.multiple_of(peer * piece, piece), piece)] if src is not cnt else src,
                dst_ref=dst.at[pl.ds(pl.multiple_of(place * piece, piece), piece)],
                send_sem=ssem.at[d],
                recv_sem=rsem.at[place],
                device_id=(peer, me_h),
                device_id_type=MESH,
            ))
        return out

    def mine(piece):
        return pl.ds(pl.multiple_of(me_c * piece, piece), piece)

    def head_rows(h):
        return pl.ds(pl.multiple_of(h * DH, DH), DH)

    def scan(got_ref, pre_ref, backward):
        total = jnp.zeros((pr, DH), F32)
        order = range(n_ctx - 1, -1, -1) if backward else range(n_ctx)
        for j in order:
            block = slice(j * pr, (j + 1) * pr)
            pre_ref[block, :] = total.astype(BF16)
            total = total + got_ref[block, :].astype(F32)

    def start(copies):
        for one in copies:
            one.start()

    def finish_recv(copies):
        for one in copies:
            one.wait_recv()

    def finish_send(copies):
        for one in copies:
            one.wait_send()

    loads[0].wait()
    loads[1].wait()

    @pl.loop(0, heads, unroll=True)
    def _(h):
        cols = lanes(h * DH, DH)
        loc[head_rows(h), :] = dot(k[:, cols], v[:, cols], TN).astype(BF16)

    loads[3].start()
    loads[4].start()
    flags = valid_ref[...].astype(F32)
    cnt[...] = jnp.zeros_like(cnt) + jnp.sum(flags)
    pl.semaphore_wait(barrier, n_ctx - 1 + 3)

    a_send = peers(True, loc, got, a_s, a_r, pr)
    n_send = peers(True, cnt, cnts, n_s, n_r, 8)
    start(a_send)
    start(n_send)
    got[mine(pr), :] = loc[mine(pr), :]
    cnts[mine(8), :] = cnt[...]

    loads[2].wait()
    row = lax.broadcasted_iota(jnp.int32, (half, half), 0)
    col = lax.broadcasted_iota(jnp.int32, (half, half), 1)
    lower = row >= col
    upper = row <= col

    def both(ref, cols):
        return ref[0:half, cols], ref[half:rows, cols]

    def full(a, b):
        return dot(a, b, NT).astype(BF16)

    def tri(a, b, mask):
        return jnp.where(mask, dot(a, b, NT), 0.0).astype(BF16)

    @pl.loop(0, heads, unroll=2)
    def _(h):
        cols = lanes(h * DH, DH)
        (k0, k1), (v0, v1), (q0, q1) = both(k, cols), both(v, cols), both(q, cols)
        intra[0:half, cols] = dot(tri(q0, k0, lower), v0, NN)
        intra[half:rows, cols] = dot(full(q1, k0), v0, NN) + dot(tri(q1, k1, lower), v1, NN)

    finish_recv(peers(False, loc, got, a_s, a_r, pr))
    scan(got, pre, False)
    b_send = peers(True, pre, state, b_s, b_r, pr)
    start(b_send)
    state[mine(pr), :] = pre[mine(pr), :]
    finish_send(a_send)
    finish_send(n_send)
    finish_recv(peers(False, cnt, cnts, n_s, n_r, 8))
    count = cnts[0:8, :]
    for j in range(1, n_ctx):
        count = count + cnts[j * 8 : j * 8 + 8, :]
    factor = (tokens / count)[0:1, :]
    diagonal = row[0:DH, 0:DH] == col[0:DH, 0:DH]
    for j in range(rows // DH):
        column = jnp.sum(jnp.where(diagonal, flags[j : j + 1, :], 0.0), axis=1, keepdims=True)
        weight[j * DH : (j + 1) * DH, :] = column * factor
    loads[3].wait()
    loads[4].wait()
    finish_recv(peers(False, pre, state, b_s, b_r, pr))

    def attend(base):
        at = pl.ds(base, half)

        @pl.loop(0, heads, unroll=True)
        def _(h):
            cols = lanes(h * DH, DH)
            carried = dot(q[at, cols], state[head_rows(h), :], NN)
            attn[at, cols] = (scale * (intra[at, cols] + carried)).astype(BF16)

    def remote(src, dst, ssem, rsem, device):
        return pltpu.make_async_remote_copy(
            src_ref=src, dst_ref=dst, send_sem=ssem, recv_sem=rsem,
            device_id=(me_c, device), device_id_type=MESH)

    own = lanes(core * part, part)
    theirs = lanes((1 - core) * part, part)
    step_rows = 64
    sent = []

    def send(src, dst, ssem, rsem, n, device):
        copy = remote(src, dst, ssem.at[n], rsem.at[n], device)
        copy.start()
        sent.append(copy)
        return copy

    def quarters(c):
        return pl.ds(2 * c * quarter, quarter), pl.ds((2 * c + 1) * quarter, quarter)

    near_r, near_l, far = (x + 1) % n_x, (x + n_x - 1) % n_x, (x + 2) % n_x
    targets = [far, near_r, near_l, x]
    t_copies, x_copies = {}, {}

    def first_terms():
        at = pl.ds(0, half)
        for mine_too in (0, 1):
            here = (1 - core if mine_too == 0 else core) * part
            lo = 0
            while lo < part:
                size = min(256, part - lo)
                tp[0, at, lanes(here + lo, size)] = dot(
                    attn[at, :], w[:, lanes(far * wide + here + lo, size)], NN).astype(BF16)
                lo += size
            if mine_too == 0:
                t_copies[0, 0] = send(tp.at[0, at, theirs], trecv.at[0, at, :], t_s, t_r, 0, other)

    def terms(i, c):
        at = pl.ds(c * half, half)
        base = targets[i] * wide

        @pl.loop(0, wide // 256, unroll=UT)
        def _(n):
            tp[i, at, lanes(n * 256, 256)] = dot(attn[at, :], w[:, lanes(base + n * 256, 256)], NN).astype(BF16)

        t_copies[i, c] = send(tp.at[i, at, theirs], trecv.at[i, at, :], t_s, t_r, 4 * c + i, other)

    def add_chip(i, c):
        t_copies[i, c].wait_recv()

        @pl.loop(0, half // step_rows)
        def _(r):
            at = pl.ds(pl.multiple_of(c * half + r * step_rows, step_rows), step_rows)
            tp[i, at, own] = (tp[i, at, own].astype(F32) + trecv[i, at, :].astype(F32)).astype(BF16)

    def add_relay(i, rel, c, base):
        @pl.loop(0, quarter // step_rows)
        def _(r):
            off = pl.multiple_of(r * step_rows, step_rows)
            at = pl.ds(base + off, step_rows)
            tp[i, at, own] = (tp[i, at, own].astype(F32) + rel[c, pl.ds(off, step_rows), :].astype(F32)).astype(BF16)

    def send_x(n, c, src, dst, device):
        x_copies[n, c] = send(src, dst, x_s, x_r, 6 * c + n, device)

    def far_out(c):
        qa, qb = quarters(c)
        add_chip(0, c)
        send_x(0, c, tp.at[0, qa, own], relay_p.at[c], right)
        send_x(1, c, tp.at[0, qb, own], relay_m.at[c], left)

    def right_out(c):
        qa, qb = quarters(c)
        add_chip(1, c)
        send_x(2, c, tp.at[1, qb, own], fin_p.at[qb], right)

    def left_out(c):
        qa, qb = quarters(c)
        add_chip(2, c)
        send_x(3, c, tp.at[2, qa, own], fin_m.at[qa], left)

    def relayed(c):
        qa, qb = quarters(c)
        x_copies[0, c].wait_recv()
        add_relay(1, relay_p, c, 2 * c * quarter)
        send_x(4, c, tp.at[1, qa, own], fin_p.at[qa], right)
        x_copies[1, c].wait_recv()
        add_relay(2, relay_m, c, (2 * c + 1) * quarter)
        send_x(5, c, tp.at[2, qb, own], fin_m.at[qb], left)

    def to_other(n, c, block, at):
        ref = gath.at[block, at, own]
        send(ref, ref, gp_s, gp_r, 7 * c + n, other)

    def from_other(n, c, block, at):
        ref = gath.at[block, at, theirs]
        remote(ref, ref, gp_s.at[7 * c + n], gp_r.at[7 * c + n], other).wait_recv()

    def to_x(n, c, block, at, device):
        ref = gath.at[block, at, own]
        send(ref, ref, gx_s, gx_r, 6 * c + n, device)

    def from_x(n, c, block, at, device):
        ref = gath.at[block, at, own]
        remote(ref, ref, gx_s.at[6 * c + n], gx_r.at[6 * c + n], device).wait_recv()

    def error(c):
        t_copies[3, c].wait_recv()
        for n in (2, 3, 4, 5):
            x_copies[n, c].wait_recv()

        @pl.loop(0, half // step_rows)
        def _(r):
            at = pl.ds(pl.multiple_of(c * half + r * step_rows, step_rows), step_rows)
            pred = tp[3, at, own].astype(F32) + trecv[3, at, :].astype(F32)
            pred = pred + fin_p[at, :].astype(F32) + fin_m[at, :].astype(F32)
            miss = pred - teacher[at, :].astype(F32)
            gath[x, at, own] = (miss * jnp.concatenate([weight[at, :]] * (part // DH), axis=1)).astype(BF16)

        qa, qb = quarters(c)
        to_x(0, c, x, qa, right)
        to_x(1, c, x, qb, left)
        to_x(2, c, x, qb, right)
        to_x(3, c, x, qa, left)
        to_other(0, c, x, pl.ds(c * half, half))

    def near_first(c):
        qa, qb = quarters(c)
        from_x(0, c, near_l, qa, left)
        to_x(4, c, near_l, qa, right)
        to_other(1, c, near_l, qa)
        from_x(1, c, near_r, qb, right)
        to_x(5, c, near_r, qb, left)
        to_other(2, c, near_r, qb)

    def near_second(c):
        qa, qb = quarters(c)
        from_x(2, c, near_l, qb, left)
        to_other(3, c, near_l, qb)
        from_x(3, c, near_r, qa, right)
        to_other(4, c, near_r, qa)

    def far_in(c):
        qa, qb = quarters(c)
        from_x(4, c, far, qa, left)
        to_other(5, c, far, qa)
        from_x(5, c, far, qb, right)
        to_other(6, c, far, qb)

    def contract(block, c, lo=0, size=wide, fresh=False):
        at = pl.ds(c * half, half)

        @pl.loop(0, heads * DH // 256, unroll=UC)
        def _(n):
            cols = lanes(n * 256, 256)
            new = dot(
                gath[block, at, lanes(lo, size)],
                w[lanes(n * 256, 256), lanes(block * wide + lo, size)],
                NT,
            )
            acc[at, cols] = new if fresh else acc[at, cols] + new

    def contract_own(c):
        from_other(0, c, x, pl.ds(c * half, half))
        contract(x, c, fresh=True)

    def contract_near(c):
        qa, qb = quarters(c)
        from_other(1, c, near_l, qa)
        from_other(3, c, near_l, qb)
        contract(near_l, c)
        from_other(2, c, near_r, qb)
        from_other(4, c, near_r, qa)
        contract(near_r, c)

    def contract_far(c):
        qa, qb = quarters(c)
        contract(far, c, core * part, part)
        from_other(5, c, far, qa)
        from_other(6, c, far, qb)
        contract(far, c, (1 - core) * part, part)

    attend(0)
    first_terms()
    terms(1, 0)
    far_out(0)
    terms(2, 0)
    right_out(0)
    terms(3, 0)
    left_out(0)
    attend(half)
    terms(0, 1)
    relayed(0)
    terms(1, 1)
    far_out(1)
    terms(2, 1)
    right_out(1)
    terms(3, 1)
    left_out(1)
    error(0)
    relayed(1)
    contract_own(0)
    near_first(0)
    near_second(0)
    contract_near(0)
    error(1)
    contract_own(1)
    far_in(0)
    contract_far(0)

    @pl.loop(0, heads, unroll=True)
    def _(h):
        cols = lanes(h * DH, DH)
        g_h = acc[0:half, cols].astype(BF16)
        g[0:half, cols] = g_h
        acc[0:DH, cols] = dot(q[0:half, cols], g_h, TN)

    near_first(1)
    near_second(1)
    contract_near(1)
    far_in(1)
    contract_far(1)

    @pl.loop(0, heads, unroll=True)
    def _(h):
        cols = lanes(h * DH, DH)
        g_h = acc[half:rows, cols].astype(BF16)
        g[half:rows, cols] = g_h
        loc2[head_rows(h), :] = (acc[0:DH, cols] + dot(q[half:rows, cols], g_h, TN)).astype(BF16)

    c_send = peers(True, loc2, got2, c_s, c_r, pr)
    start(c_send)
    got2[mine(pr), :] = loc2[mine(pr), :]

    outs = []

    def block_gradients(lo, hi):
        @pl.loop(lo, hi, unroll=UG)
        def _(h):
            cols = lanes(h * DH, DH)
            (k0, k1), (v0, v1), (q0, q1), (g0, g1) = both(k, cols), both(v, cols), both(q, cols), both(g, cols)
            p = state[head_rows(h), :]
            dq[0:half, cols] = (dot(tri(g0, v0, lower), k0, NN) + dot(g0, p, NT)).astype(BF16)
            dq[half:rows, cols] = (
                dot(full(g1, v0), k0, NN) + dot(tri(g1, v1, lower), k1, NN) + dot(g1, p, NT)
            ).astype(BF16)
            dk[0:half, cols] = (dot(tri(v0, g0, upper), q0, NN) + dot(full(v0, g1), q1, NN)).astype(BF16)
            dk[half:rows, cols] = dot(tri(v1, g1, upper), q1, NN).astype(BF16)
            dv[0:half, cols] = (dot(tri(k0, q0, upper), g0, NN) + dot(full(k0, q1), g1, NN)).astype(BF16)
            dv[half:rows, cols] = dot(tri(k1, q1, upper), g1, NN).astype(BF16)

        cols = pl.ds(lo * DH, (hi - lo) * DH)
        for src, dst in ((dq, dq_out), (dk, dk_out), (dv, dv_out)):
            copy = pltpu.make_async_copy(src.at[:, cols], dst.at[:, cols], out_sem.at[len(outs)])
            copy.start()
            outs.append(copy)

    block_gradients(0, heads // 2)
    finish_recv(peers(False, loc2, got2, c_s, c_r, pr))
    scan(got2, pre2, True)
    d_send = peers(True, pre2, state2, d_s, d_r, pr)
    start(d_send)
    state2[mine(pr), :] = pre2[mine(pr), :]
    block_gradients(heads // 2, heads)
    finish_send(b_send)
    finish_send(sent)
    finish_send(c_send)
    finish_recv(peers(False, pre2, state2, d_s, d_r, pr))
    last = pltpu.make_async_copy(state2, suffix_out, out_sem.at[6])
    last.start()
    finish_send(d_send)
    for one in outs:
        one.wait()
    last.wait()


def gradients(scale, k_ref, v_ref, pq_ref, pk_ref, pv_ref, r_ref, dq_ref, dk_ref, dv_ref):
    for h in range(k_ref.shape[1] // DH):
        cols = slice(h * DH, (h + 1) * DH)
        r = r_ref[cols, :]
        dq_ref[:, cols] = scale * pq_ref[:, cols].astype(F32)
        dk_ref[:, cols] = scale * (pk_ref[:, cols].astype(F32) + dot(v_ref[:, cols], r, NT))
        dv_ref[:, cols] = scale * (pv_ref[:, cols].astype(F32) + dot(k_ref[:, cols], r, NN))


def on_device(queries, keys, values, teacher, out_weight, valid):
    rows, width = queries.shape
    heads = width // DH
    model = out_weight.shape[1]
    n_ctx = lax.axis_size("ctx")
    n_x = lax.axis_size("head") // 2
    half = rows // 2
    wide = model // n_x
    part = wide // 2
    tokens = float(rows * n_ctx)
    scale = 1.0 / math.sqrt(DH * rows * n_ctx)
    valid_rows = valid.reshape(rows // DH, DH)
    anywhere = pl.BlockSpec(memory_space=pl.ANY)
    vmem = pl.BlockSpec(memory_space=pltpu.VMEM)
    dma = pltpu.SemaphoreType.DMA
    st = lambda: pltpu.VMEM((heads * DH, DH), BF16)
    whole = jax.ShapeDtypeStruct((rows, width), BF16)
    dq, dk, dv, suffix = pl.pallas_call(
        functools.partial(transfer, scale, heads, n_ctx, n_x, tokens),
        name="transfer",
        out_shape=(whole, whole, whole, jax.ShapeDtypeStruct((width, DH), BF16)),
        in_specs=[anywhere] * 5 + [vmem],
        out_specs=(anywhere,) * 4,
        scratch_shapes=[
            pltpu.VMEM((rows, width), BF16),
            pltpu.VMEM((rows, width), BF16),
            pltpu.VMEM((rows, width), BF16),
            pltpu.VMEM((rows, part), BF16),
            pltpu.VMEM((width, model), BF16),
            pltpu.VMEM((rows, width), F32),
            pltpu.VMEM((rows, width), BF16),
            pltpu.VMEM((4, rows, wide), BF16),
            pltpu.VMEM((4, rows, part), BF16),
            pltpu.VMEM((2, half // 2, part), BF16),
            pltpu.VMEM((2, half // 2, part), BF16),
            pltpu.VMEM((rows, part), BF16),
            pltpu.VMEM((rows, part), BF16),
            pltpu.VMEM((n_x, rows, wide), BF16),
            pltpu.VMEM((rows, width), F32),
            pltpu.VMEM((rows, width), BF16),
            pltpu.VMEM((rows, width), BF16),
            pltpu.VMEM((rows, width), BF16),
            pltpu.VMEM((rows, width), BF16),
            pltpu.VMEM((rows, DH), F32),
            st(), st(), st(), st(), st(), st(), st(), st(),
            pltpu.VMEM((8, 128), F32),
            pltpu.VMEM((8 * n_ctx, 128), F32),
            dma((5,)), dma((7,)),
            dma((n_ctx,)), dma((n_ctx,)), dma((n_ctx,)), dma((n_ctx,)),
            dma((n_ctx,)), dma((n_ctx,)), dma((n_ctx,)), dma((n_ctx,)),
            dma((n_ctx,)), dma((n_ctx,)),
            dma((8,)), dma((8,)), dma((12,)), dma((12,)),
            dma((14,)), dma((14,)), dma((12,)), dma((12,)),
        ],
        compiler_params=pltpu.CompilerParams(
            collective_id=0, has_side_effects=True, vmem_limit_bytes=60 * 1024 * 1024
        ),
    )(queries, keys, values, teacher, out_weight, valid_rows)

    per = 4
    block = pl.BlockSpec((rows, per * DH), lambda i: (0, i))
    square = pl.BlockSpec((per * DH, DH), lambda i: (i, 0))
    return tuple(pl.pallas_call(
        functools.partial(gradients, scale),
        name="gradients",
        grid=(heads // per,),
        out_shape=(jax.ShapeDtypeStruct((rows, width), F32),) * 3,
        in_specs=[block] * 5 + [square],
        out_specs=(block,) * 3,
    )(keys, values, dq, dk, dv, suffix))


def solution(mesh):
    in_specs = (
        P("ctx", "head"),
        P("ctx", "head"),
        P("ctx", "head"),
        P("ctx", "head"),
        P("head", None),
        P("ctx"),
    )
    out_specs = (P("ctx", "head"), P("ctx", "head"), P("ctx", "head"))
    return jax.shard_map(
        on_device, mesh=mesh, in_specs=in_specs, out_specs=out_specs, check_vma=False
    )
```

```python
import functools
import math

import jax
import jax.numpy as jnp
from jax import lax
from jax.experimental import pallas as pl
from jax.experimental.pallas import tpu as pltpu
from jax.sharding import PartitionSpec as P

DH = 128
UT = True
UC = True
UG = 2
LIMIT = 54
MESH = pl.DeviceIdType.MESH
F32 = jnp.float32
BF16 = jnp.bfloat16
NT = (((1,), (1,)), ((), ()))
TN = (((0,), (0,)), ((), ()))
NN = (((1,), (0,)), ((), ()))


def dot(a, b, dims):
    return lax.dot_general(a, b, dims, preferred_element_type=F32)


def lanes(start, size):
    return pl.ds(pl.multiple_of(start, 128), size)


def transfer(scale, heads, n_ctx, n_x, tokens,
             q_hbm, k_hbm, v_hbm, teacher_hbm, w_hbm, valid_ref,
             k, v, dq, dk, dv, suffix,
             q, teacher, w, intra, attn, tp, trecv, relay_p, relay_m, fin_p, fin_m,
             gath, acc, g, weight, loc, got, pre, state, loc2, got2, pre2, state2, cnt, cnts,
             in_sem, a_s, a_r, b_s, b_r, c_s, c_r, d_s, d_r, n_s, n_r,
             t_s, t_r, x_s, x_r, gp_s, gp_r, gx_s, gx_r):
    rows = q.shape[0]
    half = rows // 2
    quarter = rows // 4
    wide = w.shape[1] // n_x
    part = wide // 2
    me_c = lax.axis_index("ctx")
    me_h = lax.axis_index("head")
    x, core = me_h // 2, me_h % 2
    right = ((x + 1) % n_x) * 2 + core
    left = ((x + n_x - 1) % n_x) * 2 + core
    other = x * 2 + 1 - core
    pr = heads * DH // n_ctx

    barrier = pltpu.get_barrier_semaphore()
    for d in range(1, n_ctx):
        pl.semaphore_signal(barrier, inc=1, device_id=((me_c + d) % n_ctx, me_h), device_id_type=MESH)
    for h in (other, right, left):
        pl.semaphore_signal(barrier, inc=1, device_id=(me_c, h), device_id_type=MESH)

    loads = [
        pltpu.make_async_copy(src, dst, in_sem.at[i])
        for i, (src, dst) in enumerate(((k_hbm, k), (v_hbm, v), (q_hbm, q), (w_hbm, w), (teacher_hbm, teacher)))
    ]
    for one in loads[:3]:
        one.start()

    n_y = math.isqrt(n_ctx) if math.isqrt(n_ctx) ** 2 == n_ctx else n_ctx
    n_z = n_ctx // n_y
    offsets = sorted(
        ((i, j) for i in range(n_z) for j in range(n_y) if i or j),
        key=lambda o: -min(o[0], n_z - o[0]) - min(o[1], n_y - o[1]),
    )

    def peers(sending, src, dst, ssem, rsem, piece):
        out = []
        for d, (oz, oy) in enumerate(offsets):
            if not sending:
                oz, oy = n_z - oz, n_y - oy
            peer = ((me_c // n_y + oz) % n_z) * n_y + (me_c % n_y + oy) % n_y
            place = me_c if sending else peer
            out.append(pltpu.make_async_remote_copy(
                src_ref=src.at[pl.ds(pl.multiple_of(peer * piece, piece), piece)] if src is not cnt else src,
                dst_ref=dst.at[pl.ds(pl.multiple_of(place * piece, piece), piece)],
                send_sem=ssem.at[d],
                recv_sem=rsem.at[place],
                device_id=(peer, me_h),
                device_id_type=MESH,
            ))
        return out

    def mine(piece):
        return pl.ds(pl.multiple_of(me_c * piece, piece), piece)

    def head_rows(h):
        return pl.ds(pl.multiple_of(h * DH, DH), DH)

    def scan(got_ref, pre_ref, backward):
        total = jnp.zeros((pr, DH), F32)
        order = range(n_ctx - 1, -1, -1) if backward else range(n_ctx)
        for j in order:
            block = slice(j * pr, (j + 1) * pr)
            pre_ref[block, :] = total.astype(BF16)
            total = total + got_ref[block, :].astype(F32)

    def start(copies):
        for one in copies:
            one.start()

    def finish_recv(copies):
        for one in copies:
            one.wait_recv()

    def finish_send(copies):
        for one in copies:
            one.wait_send()

    loads[0].wait()
    loads[1].wait()

    @pl.loop(0, heads, unroll=True)
    def _(h):
        cols = lanes(h * DH, DH)
        loc[head_rows(h), :] = dot(k[:, cols], v[:, cols], TN).astype(BF16)

    loads[3].start()
    loads[4].start()
    flags = valid_ref[...].astype(F32)
    cnt[...] = jnp.zeros_like(cnt) + jnp.sum(flags)
    pl.semaphore_wait(barrier, n_ctx - 1 + 3)

    a_send = peers(True, loc, got, a_s, a_r, pr)
    n_send = peers(True, cnt, cnts, n_s, n_r, 8)
    start(a_send)
    start(n_send)
    got[mine(pr), :] = loc[mine(pr), :]
    cnts[mine(8), :] = cnt[...]

    loads[2].wait()
    row = lax.broadcasted_iota(jnp.int32, (half, half), 0)
    col = lax.broadcasted_iota(jnp.int32, (half, half), 1)
    lower = row >= col
    upper = row <= col

    def both(ref, cols):
        return ref[0:half, cols], ref[half:rows, cols]

    def full(a, b):
        return dot(a, b, NT).astype(BF16)

    def tri(a, b, mask):
        return jnp.where(mask, dot(a, b, NT), 0.0).astype(BF16)

    @pl.loop(0, heads, unroll=2)
    def _(h):
        cols = lanes(h * DH, DH)
        (k0, k1), (v0, v1), (q0, q1) = both(k, cols), both(v, cols), both(q, cols)
        intra[0:half, cols] = dot(tri(q0, k0, lower), v0, NN)
        intra[half:rows, cols] = dot(full(q1, k0), v0, NN) + dot(tri(q1, k1, lower), v1, NN)

    finish_recv(peers(False, loc, got, a_s, a_r, pr))
    scan(got, pre, False)
    b_send = peers(True, pre, state, b_s, b_r, pr)
    start(b_send)
    state[mine(pr), :] = pre[mine(pr), :]
    finish_send(a_send)
    finish_send(n_send)
    finish_recv(peers(False, cnt, cnts, n_s, n_r, 8))
    count = cnts[0:8, :]
    for j in range(1, n_ctx):
        count = count + cnts[j * 8 : j * 8 + 8, :]
    factor = (tokens / count)[0:1, :]
    diagonal = row[0:DH, 0:DH] == col[0:DH, 0:DH]
    for j in range(rows // DH):
        column = jnp.sum(jnp.where(diagonal, flags[j : j + 1, :], 0.0), axis=1, keepdims=True)
        weight[j * DH : (j + 1) * DH, :] = column * factor
    loads[3].wait()
    loads[4].wait()
    finish_recv(peers(False, pre, state, b_s, b_r, pr))

    def attend(base):
        at = pl.ds(base, half)

        @pl.loop(0, heads, unroll=True)
        def _(h):
            cols = lanes(h * DH, DH)
            carried = dot(q[at, cols], state[head_rows(h), :], NN)
            attn[at, cols] = (scale * (intra[at, cols] + carried)).astype(BF16)

    def remote(src, dst, ssem, rsem, device):
        return pltpu.make_async_remote_copy(
            src_ref=src, dst_ref=dst, send_sem=ssem, recv_sem=rsem,
            device_id=(me_c, device), device_id_type=MESH)

    own = lanes(core * part, part)
    theirs = lanes((1 - core) * part, part)
    step_rows = 64
    sent = []

    def send(src, dst, ssem, rsem, n, device):
        copy = remote(src, dst, ssem.at[n], rsem.at[n], device)
        copy.start()
        sent.append(copy)
        return copy

    def quarters(c):
        return pl.ds(2 * c * quarter, quarter), pl.ds((2 * c + 1) * quarter, quarter)

    near_r, near_l, far = (x + 1) % n_x, (x + n_x - 1) % n_x, (x + 2) % n_x
    targets = [far, near_r, near_l, x]
    t_copies, x_copies = {}, {}

    def first_terms():
        at = pl.ds(0, half)
        for mine_too in (0, 1):
            here = (1 - core if mine_too == 0 else core) * part
            lo = 0
            while lo < part:
                size = min(256, part - lo)
                tp[0, at, lanes(here + lo, size)] = dot(
                    attn[at, :], w[:, lanes(far * wide + here + lo, size)], NN).astype(BF16)
                lo += size
            if mine_too == 0:
                t_copies[0, 0] = send(tp.at[0, at, theirs], trecv.at[0, at, :], t_s, t_r, 0, other)

    def terms(i, c):
        at = pl.ds(c * half, half)
        base = targets[i] * wide

        @pl.loop(0, wide // 256, unroll=UT)
        def _(n):
            tp[i, at, lanes(n * 256, 256)] = dot(attn[at, :], w[:, lanes(base + n * 256, 256)], NN).astype(BF16)

        t_copies[i, c] = send(tp.at[i, at, theirs], trecv.at[i, at, :], t_s, t_r, 4 * c + i, other)

    def add_chip(i, c):
        t_copies[i, c].wait_recv()

        @pl.loop(0, half // step_rows)
        def _(r):
            at = pl.ds(pl.multiple_of(c * half + r * step_rows, step_rows), step_rows)
            tp[i, at, own] = (tp[i, at, own].astype(F32) + trecv[i, at, :].astype(F32)).astype(BF16)

    def add_relay(i, rel, c, base):
        @pl.loop(0, quarter // step_rows)
        def _(r):
            off = pl.multiple_of(r * step_rows, step_rows)
            at = pl.ds(base + off, step_rows)
            tp[i, at, own] = (tp[i, at, own].astype(F32) + rel[c, pl.ds(off, step_rows), :].astype(F32)).astype(BF16)

    def send_x(n, c, src, dst, device):
        x_copies[n, c] = send(src, dst, x_s, x_r, 6 * c + n, device)

    def far_out(c):
        qa, qb = quarters(c)
        add_chip(0, c)
        send_x(0, c, tp.at[0, qa, own], relay_p.at[c], right)
        send_x(1, c, tp.at[0, qb, own], relay_m.at[c], left)

    def right_out(c):
        qa, qb = quarters(c)
        add_chip(1, c)
        send_x(2, c, tp.at[1, qb, own], fin_p.at[qb], right)

    def left_out(c):
        qa, qb = quarters(c)
        add_chip(2, c)
        send_x(3, c, tp.at[2, qa, own], fin_m.at[qa], left)

    def relayed(c):
        qa, qb = quarters(c)
        x_copies[0, c].wait_recv()
        add_relay(1, relay_p, c, 2 * c * quarter)
        send_x(4, c, tp.at[1, qa, own], fin_p.at[qa], right)
        x_copies[1, c].wait_recv()
        add_relay(2, relay_m, c, (2 * c + 1) * quarter)
        send_x(5, c, tp.at[2, qb, own], fin_m.at[qb], left)

    def to_other(n, c, block, at):
        ref = gath.at[block, at, own]
        send(ref, ref, gp_s, gp_r, 7 * c + n, other)

    def from_other(n, c, block, at):
        ref = gath.at[block, at, theirs]
        remote(ref, ref, gp_s.at[7 * c + n], gp_r.at[7 * c + n], other).wait_recv()

    def to_x(n, c, block, at, device):
        ref = gath.at[block, at, own]
        send(ref, ref, gx_s, gx_r, 6 * c + n, device)

    def from_x(n, c, block, at, device):
        ref = gath.at[block, at, own]
        remote(ref, ref, gx_s.at[6 * c + n], gx_r.at[6 * c + n], device).wait_recv()

    def error(c):
        t_copies[3, c].wait_recv()
        for n in (2, 3, 4, 5):
            x_copies[n, c].wait_recv()

        @pl.loop(0, half // step_rows)
        def _(r):
            at = pl.ds(pl.multiple_of(c * half + r * step_rows, step_rows), step_rows)
            pred = tp[3, at, own].astype(F32) + trecv[3, at, :].astype(F32)
            pred = pred + fin_p[at, :].astype(F32) + fin_m[at, :].astype(F32)
            miss = pred - teacher[at, :].astype(F32)
            gath[x, at, own] = (miss * jnp.concatenate([weight[at, :]] * (part // DH), axis=1)).astype(BF16)

        qa, qb = quarters(c)
        to_x(0, c, x, qa, right)
        to_x(1, c, x, qb, left)
        to_x(2, c, x, qb, right)
        to_x(3, c, x, qa, left)
        to_other(0, c, x, pl.ds(c * half, half))

    def near_first(c):
        qa, qb = quarters(c)
        from_x(0, c, near_l, qa, left)
        to_x(4, c, near_l, qa, right)
        to_other(1, c, near_l, qa)
        from_x(1, c, near_r, qb, right)
        to_x(5, c, near_r, qb, left)
        to_other(2, c, near_r, qb)

    def near_second(c):
        qa, qb = quarters(c)
        from_x(2, c, near_l, qb, left)
        to_other(3, c, near_l, qb)
        from_x(3, c, near_r, qa, right)
        to_other(4, c, near_r, qa)

    def far_in(c):
        qa, qb = quarters(c)
        from_x(4, c, far, qa, left)
        to_other(5, c, far, qa)
        from_x(5, c, far, qb, right)
        to_other(6, c, far, qb)

    def contract(block, c, lo=0, size=wide, fresh=False):
        at = pl.ds(c * half, half)

        @pl.loop(0, heads * DH // 256, unroll=UC)
        def _(n):
            cols = lanes(n * 256, 256)
            new = dot(
                gath[block, at, lanes(lo, size)],
                w[lanes(n * 256, 256), lanes(block * wide + lo, size)],
                NT,
            )
            acc[at, cols] = new if fresh else acc[at, cols] + new

    def contract_own(c):
        from_other(0, c, x, pl.ds(c * half, half))
        contract(x, c, fresh=True)

    def contract_near(c):
        qa, qb = quarters(c)
        from_other(1, c, near_l, qa)
        from_other(3, c, near_l, qb)
        contract(near_l, c)
        from_other(2, c, near_r, qb)
        from_other(4, c, near_r, qa)
        contract(near_r, c)

    def contract_far(c):
        qa, qb = quarters(c)
        contract(far, c, core * part, part)
        from_other(5, c, far, qa)
        from_other(6, c, far, qb)
        contract(far, c, (1 - core) * part, part)

    attend(0)
    first_terms()
    terms(1, 0)
    far_out(0)
    terms(2, 0)
    right_out(0)
    terms(3, 0)
    left_out(0)
    attend(half)
    terms(0, 1)
    relayed(0)
    terms(1, 1)
    far_out(1)
    terms(2, 1)
    right_out(1)
    terms(3, 1)
    left_out(1)
    error(0)
    relayed(1)
    contract_own(0)
    near_first(0)
    near_second(0)
    contract_near(0)
    error(1)
    contract_own(1)
    far_in(0)
    contract_far(0)

    @pl.loop(0, heads, unroll=True)
    def _(h):
        cols = lanes(h * DH, DH)
        g_h = acc[0:half, cols].astype(BF16)
        g[0:half, cols] = g_h
        acc[0:DH, cols] = dot(q[0:half, cols], g_h, TN)

    near_first(1)
    near_second(1)
    contract_near(1)
    far_in(1)
    contract_far(1)

    @pl.loop(0, heads, unroll=True)
    def _(h):
        cols = lanes(h * DH, DH)
        g_h = acc[half:rows, cols].astype(BF16)
        g[half:rows, cols] = g_h
        loc2[head_rows(h), :] = (acc[0:DH, cols] + dot(q[half:rows, cols], g_h, TN)).astype(BF16)

    c_send = peers(True, loc2, got2, c_s, c_r, pr)
    start(c_send)
    got2[mine(pr), :] = loc2[mine(pr), :]

    def block_gradients(lo, hi):
        @pl.loop(lo, hi, unroll=UG)
        def _(h):
            cols = lanes(h * DH, DH)
            (k0, k1), (v0, v1), (q0, q1), (g0, g1) = both(k, cols), both(v, cols), both(q, cols), both(g, cols)
            p = state[head_rows(h), :]
            dq[0:half, cols] = scale * (dot(tri(g0, v0, lower), k0, NN) + dot(g0, p, NT))
            dq[half:rows, cols] = scale * (
                dot(full(g1, v0), k0, NN) + dot(tri(g1, v1, lower), k1, NN) + dot(g1, p, NT)
            )
            dk[0:half, cols] = dot(tri(v0, g0, upper), q0, NN) + dot(full(v0, g1), q1, NN)
            dk[half:rows, cols] = dot(tri(v1, g1, upper), q1, NN)
            dv[0:half, cols] = dot(tri(k0, q0, upper), g0, NN) + dot(full(k0, q1), g1, NN)
            dv[half:rows, cols] = dot(tri(k1, q1, upper), g1, NN)

    block_gradients(0, heads // 2)
    finish_recv(peers(False, loc2, got2, c_s, c_r, pr))
    scan(got2, pre2, True)
    d_send = peers(True, pre2, state2, d_s, d_r, pr)
    start(d_send)
    state2[mine(pr), :] = pre2[mine(pr), :]
    block_gradients(heads // 2, heads)
    finish_send(b_send)
    finish_send(sent)
    finish_send(c_send)
    finish_recv(peers(False, pre2, state2, d_s, d_r, pr))
    suffix[...] = state2[...]
    finish_send(d_send)


def gradients(scale, k, v, dq, pk, pv, suffix, dq_out, dk_out, dv_out, dk, dv, sems):
    heads = k.shape[1] // DH
    step = 2
    copies = [pltpu.make_async_copy(dq, dq_out, sems.at[heads])]
    copies[0].start()
    for group in range(heads // step):
        for h in range(group * step, (group + 1) * step):
            cols = slice(h * DH, (h + 1) * DH)
            r = suffix[cols, :]
            dk[:, cols] = scale * (pk[:, cols] + dot(v[:, cols], r, NT))
            dv[:, cols] = scale * (pv[:, cols] + dot(k[:, cols], r, NN))
        span = pl.ds(group * step * DH, step * DH)
        for n, (src, dst) in enumerate(((dk, dk_out), (dv, dv_out))):
            copy = pltpu.make_async_copy(src.at[:, span], dst.at[:, span], sems.at[2 * group + n])
            copy.start()
            copies.append(copy)
    for copy in copies:
        copy.wait()


def on_device(queries, keys, values, teacher, out_weight, valid):
    rows, width = queries.shape
    heads = width // DH
    model = out_weight.shape[1]
    n_ctx = lax.axis_size("ctx")
    n_x = lax.axis_size("head") // 2
    half = rows // 2
    wide = model // n_x
    part = wide // 2
    tokens = float(rows * n_ctx)
    scale = 1.0 / math.sqrt(DH * rows * n_ctx)
    valid_rows = valid.reshape(rows // DH, DH)
    anywhere = pl.BlockSpec(memory_space=pl.ANY)
    vmem = pl.BlockSpec(memory_space=pltpu.VMEM)
    dma = pltpu.SemaphoreType.DMA
    st = lambda: pltpu.VMEM((heads * DH, DH), BF16)
    kept = pltpu.VMEM((rows, width), BF16)
    passed = pl.pallas_call(
        functools.partial(transfer, scale, heads, n_ctx, n_x, tokens),
        name="transfer",
        out_shape=(kept,) * 2 + (pltpu.VMEM((rows, width), F32),) * 3 + (pltpu.VMEM((width, DH), BF16),),
        in_specs=[anywhere] * 5 + [vmem],
        out_specs=(vmem,) * 6,
        scratch_shapes=[
            pltpu.VMEM((rows, width), BF16),
            pltpu.VMEM((rows, part), BF16),
            pltpu.VMEM((width, model), BF16),
            pltpu.VMEM((rows, width), F32),
            pltpu.VMEM((rows, width), BF16),
            pltpu.VMEM((4, rows, wide), BF16),
            pltpu.VMEM((4, rows, part), BF16),
            pltpu.VMEM((2, half // 2, part), BF16),
            pltpu.VMEM((2, half // 2, part), BF16),
            pltpu.VMEM((rows, part), BF16),
            pltpu.VMEM((rows, part), BF16),
            pltpu.VMEM((n_x, rows, wide), BF16),
            pltpu.VMEM((rows, width), F32),
            pltpu.VMEM((rows, width), BF16),
            pltpu.VMEM((rows, DH), F32),
            st(), st(), st(), st(), st(), st(), st(), st(),
            pltpu.VMEM((8, 128), F32),
            pltpu.VMEM((8 * n_ctx, 128), F32),
            dma((5,)),
            dma((n_ctx,)), dma((n_ctx,)), dma((n_ctx,)), dma((n_ctx,)),
            dma((n_ctx,)), dma((n_ctx,)), dma((n_ctx,)), dma((n_ctx,)),
            dma((n_ctx,)), dma((n_ctx,)),
            dma((8,)), dma((8,)), dma((12,)), dma((12,)),
            dma((14,)), dma((14,)), dma((12,)), dma((12,)),
        ],
        compiler_params=pltpu.CompilerParams(
            collective_id=0, has_side_effects=True, vmem_limit_bytes=LIMIT * 1024 * 1024
        ),
    )(queries, keys, values, teacher, out_weight, valid_rows)

    return tuple(pl.pallas_call(
        functools.partial(gradients, scale),
        name="gradients",
        out_shape=(jax.ShapeDtypeStruct((rows, width), F32),) * 3,
        in_specs=[vmem] * 6,
        out_specs=(anywhere,) * 3,
        scratch_shapes=[pltpu.VMEM((rows, width), F32)] * 2 + [dma((heads + 1,))],
        compiler_params=pltpu.CompilerParams(vmem_limit_bytes=16 * 1024 * 1024),
    )(*passed))


def solution(mesh):
    in_specs = (
        P("ctx", "head"),
        P("ctx", "head"),
        P("ctx", "head"),
        P("ctx", "head"),
        P("head", None),
        P("ctx"),
    )
    out_specs = (P("ctx", "head"), P("ctx", "head"), P("ctx", "head"))
    return jax.shard_map(
        on_device, mesh=mesh, in_specs=in_specs, out_specs=out_specs, check_vma=False
    )
```

```python
import functools
import math

import jax
import jax.numpy as jnp
from jax import lax
from jax.experimental import pallas as pl
from jax.experimental.pallas import tpu as pltpu
from jax.sharding import PartitionSpec as P

DH = 128
UT = True
UC = True
UG = 2
LIMIT = 54
MESH = pl.DeviceIdType.MESH
F32 = jnp.float32
BF16 = jnp.bfloat16
NT = (((1,), (1,)), ((), ()))
TN = (((0,), (0,)), ((), ()))
NN = (((1,), (0,)), ((), ()))


def dot(a, b, dims):
    return lax.dot_general(a, b, dims, preferred_element_type=F32)


def lanes(start, size):
    return pl.ds(pl.multiple_of(start, 128), size)


def transfer(scale, heads, n_ctx, n_x, tokens,
             q_hbm, k_hbm, v_hbm, teacher_hbm, w_hbm, valid_ref,
             k, v, dq, dk, dv, suffix,
             q, teacher, w, intra, attn, tp, trecv, relay_p, relay_m, fin_p, fin_m,
             gath, acc, g, weight, loc, got, pre, state, loc2, got2, pre2, state2, cnt, cnts,
             in_sem, a_s, a_r, b_s, b_r, c_s, c_r, d_s, d_r, n_s, n_r,
             t_s, t_r, x_s, x_r, gp_s, gp_r, gx_s, gx_r):
    rows = q.shape[0]
    half = rows // 2
    quarter = rows // 4
    wide = w.shape[1] // n_x
    part = wide // 2
    me_c = lax.axis_index("ctx")
    me_h = lax.axis_index("head")
    x, core = me_h // 2, me_h % 2
    right = ((x + 1) % n_x) * 2 + core
    left = ((x + n_x - 1) % n_x) * 2 + core
    other = x * 2 + 1 - core
    pr = heads * DH // n_ctx

    barrier = pltpu.get_barrier_semaphore()
    for d in range(1, n_ctx):
        pl.semaphore_signal(barrier, inc=1, device_id=((me_c + d) % n_ctx, me_h), device_id_type=MESH)
    for h in (other, right, left):
        pl.semaphore_signal(barrier, inc=1, device_id=(me_c, h), device_id_type=MESH)

    loads = [
        pltpu.make_async_copy(src, dst, in_sem.at[i])
        for i, (src, dst) in enumerate(((k_hbm, k), (v_hbm, v), (q_hbm, q), (w_hbm, w), (teacher_hbm, teacher)))
    ]
    for one in loads[:3]:
        one.start()

    n_y = math.isqrt(n_ctx) if math.isqrt(n_ctx) ** 2 == n_ctx else n_ctx
    n_z = n_ctx // n_y
    offsets = sorted(
        ((i, j) for i in range(n_z) for j in range(n_y) if i or j),
        key=lambda o: -min(o[0], n_z - o[0]) - min(o[1], n_y - o[1]),
    )

    def peers(sending, src, dst, ssem, rsem, piece):
        out = []
        for d, (oz, oy) in enumerate(offsets):
            if not sending:
                oz, oy = n_z - oz, n_y - oy
            peer = ((me_c // n_y + oz) % n_z) * n_y + (me_c % n_y + oy) % n_y
            place = me_c if sending else peer
            out.append(pltpu.make_async_remote_copy(
                src_ref=src.at[pl.ds(pl.multiple_of(peer * piece, piece), piece)] if src is not cnt else src,
                dst_ref=dst.at[pl.ds(pl.multiple_of(place * piece, piece), piece)],
                send_sem=ssem.at[d],
                recv_sem=rsem.at[place],
                device_id=(peer, me_h),
                device_id_type=MESH,
            ))
        return out

    def mine(piece):
        return pl.ds(pl.multiple_of(me_c * piece, piece), piece)

    def head_rows(h):
        return pl.ds(pl.multiple_of(h * DH, DH), DH)

    def scan(got_ref, pre_ref, backward):
        total = jnp.zeros((pr, DH), F32)
        order = range(n_ctx - 1, -1, -1) if backward else range(n_ctx)
        for j in order:
            block = slice(j * pr, (j + 1) * pr)
            pre_ref[block, :] = total.astype(BF16)
            total = total + got_ref[block, :].astype(F32)

    def start(copies):
        for one in copies:
            one.start()

    def finish_recv(copies):
        for one in copies:
            one.wait_recv()

    def finish_send(copies):
        for one in copies:
            one.wait_send()

    loads[0].wait()
    loads[1].wait()

    @pl.loop(0, heads, unroll=True)
    def _(h):
        cols = lanes(h * DH, DH)
        loc[head_rows(h), :] = dot(k[:, cols], v[:, cols], TN).astype(BF16)

    loads[3].start()
    loads[4].start()
    cnt[...] = jnp.zeros_like(cnt) + jnp.sum(valid_ref[...].astype(F32))
    pl.semaphore_wait(barrier, n_ctx - 1 + 3)

    a_send = peers(True, loc, got, a_s, a_r, pr)
    start(a_send)
    got[mine(pr), :] = loc[mine(pr), :]
    cnts[mine(8), :] = cnt[...]

    loads[2].wait()
    row = lax.broadcasted_iota(jnp.int32, (half, half), 0)
    col = lax.broadcasted_iota(jnp.int32, (half, half), 1)
    lower = row >= col
    upper = row <= col

    def both(ref, cols):
        return ref[0:half, cols], ref[half:rows, cols]

    def full(a, b):
        return dot(a, b, NT).astype(BF16)

    def tri(a, b, mask):
        return jnp.where(mask, dot(a, b, NT), 0.0).astype(BF16)

    @pl.loop(0, heads, unroll=2)
    def _(h):
        cols = lanes(h * DH, DH)
        (k0, k1), (v0, v1), (q0, q1) = both(k, cols), both(v, cols), both(q, cols)
        intra[0:half, cols] = dot(tri(q0, k0, lower), v0, NN)
        intra[half:rows, cols] = dot(full(q1, k0), v0, NN) + dot(tri(q1, k1, lower), v1, NN)

    finish_recv(peers(False, loc, got, a_s, a_r, pr))
    scan(got, pre, False)
    b_send = peers(True, pre, state, b_s, b_r, pr)
    start(b_send)
    n_send = peers(True, cnt, cnts, n_s, n_r, 8)
    start(n_send)
    state[mine(pr), :] = pre[mine(pr), :]
    finish_send(a_send)
    loads[3].wait()
    loads[4].wait()
    finish_recv(peers(False, pre, state, b_s, b_r, pr))

    def weigh():
        finish_recv(peers(False, cnt, cnts, n_s, n_r, 8))
        count = cnts[0:8, :]
        for j in range(1, n_ctx):
            count = count + cnts[j * 8 : j * 8 + 8, :]
        factor = (tokens / count)[0:1, :]
        diagonal = row[0:DH, 0:DH] == col[0:DH, 0:DH]
        for j in range(rows // DH):
            column = jnp.sum(jnp.where(diagonal, valid_ref[j : j + 1, :].astype(F32), 0.0), axis=1, keepdims=True)
            weight[j * DH : (j + 1) * DH, :] = column * factor

    def attend(base, size):
        at = pl.ds(base, size)

        @pl.loop(0, heads, unroll=True)
        def _(h):
            cols = lanes(h * DH, DH)
            carried = dot(q[at, cols], state[head_rows(h), :], NN)
            attn[at, cols] = (scale * (intra[at, cols] + carried)).astype(BF16)

    def remote(src, dst, ssem, rsem, device):
        return pltpu.make_async_remote_copy(
            src_ref=src, dst_ref=dst, send_sem=ssem, recv_sem=rsem,
            device_id=(me_c, device), device_id_type=MESH)

    own = lanes(core * part, part)
    theirs = lanes((1 - core) * part, part)
    step_rows = 64
    sent = []

    def send(src, dst, ssem, rsem, n, device):
        copy = remote(src, dst, ssem.at[n], rsem.at[n], device)
        copy.start()
        sent.append(copy)
        return copy

    def quarters(c):
        return pl.ds(2 * c * quarter, quarter), pl.ds((2 * c + 1) * quarter, quarter)

    near_r, near_l, far = (x + 1) % n_x, (x + n_x - 1) % n_x, (x + 2) % n_x
    targets = [far, near_r, near_l, x]
    t_copies, x_copies = {}, {}

    def some_terms(at, here):
        lo = 0
        while lo < part:
            size = min(256, part - lo)
            tp[0, at, lanes(here + lo, size)] = dot(
                attn[at, :], w[:, lanes(far * wide + here + lo, size)], NN).astype(BF16)
            lo += size

    def first_terms():
        parts = quarters(0)
        copies = []
        for n, at in enumerate(parts):
            attend(n * quarter, quarter)
            some_terms(at, (1 - core) * part)
            copies.append(send(tp.at[0, at, theirs], trecv.at[0, at, :], t_s, t_r, (0, 8)[n], other))
        some_terms(pl.ds(0, half), core * part)
        for n, (at, relay, device) in enumerate(zip(parts, (relay_p, relay_m), (right, left))):
            copies[n].wait_recv()
            add_rows(0, n * quarter, quarter)
            send_x(n, 0, tp.at[0, at, own], relay.at[0], device)

    def terms(i, c):
        at = pl.ds(c * half, half)
        base = targets[i] * wide

        @pl.loop(0, wide // 256, unroll=UT)
        def _(n):
            tp[i, at, lanes(n * 256, 256)] = dot(attn[at, :], w[:, lanes(base + n * 256, 256)], NN).astype(BF16)

        t_copies[i, c] = send(tp.at[i, at, theirs], trecv.at[i, at, :], t_s, t_r, 4 * c + i, other)

    def add_chip(i, c):
        t_copies[i, c].wait_recv()
        add_rows(i, c * half, half)

    def add_rows(i, base, size):
        @pl.loop(0, size // step_rows, unroll=True)
        def _(r):
            at = pl.ds(pl.multiple_of(base + r * step_rows, step_rows), step_rows)
            tp[i, at, own] = (tp[i, at, own].astype(F32) + trecv[i, at, :].astype(F32)).astype(BF16)

    def add_relay(i, rel, c, base):
        @pl.loop(0, quarter // step_rows, unroll=True)
        def _(r):
            off = pl.multiple_of(r * step_rows, step_rows)
            at = pl.ds(base + off, step_rows)
            tp[i, at, own] = (tp[i, at, own].astype(F32) + rel[c, pl.ds(off, step_rows), :].astype(F32)).astype(BF16)

    def send_x(n, c, src, dst, device):
        x_copies[n, c] = send(src, dst, x_s, x_r, 6 * c + n, device)

    def far_out(c):
        qa, qb = quarters(c)
        add_chip(0, c)
        send_x(0, c, tp.at[0, qa, own], relay_p.at[c], right)
        send_x(1, c, tp.at[0, qb, own], relay_m.at[c], left)

    def right_out(c):
        qa, qb = quarters(c)
        add_chip(1, c)
        send_x(2, c, tp.at[1, qb, own], fin_p.at[qb], right)

    def left_out(c):
        qa, qb = quarters(c)
        add_chip(2, c)
        send_x(3, c, tp.at[2, qa, own], fin_m.at[qa], left)

    def relayed(c):
        qa, qb = quarters(c)
        x_copies[0, c].wait_recv()
        add_relay(1, relay_p, c, 2 * c * quarter)
        send_x(4, c, tp.at[1, qa, own], fin_p.at[qa], right)
        x_copies[1, c].wait_recv()
        add_relay(2, relay_m, c, (2 * c + 1) * quarter)
        send_x(5, c, tp.at[2, qb, own], fin_m.at[qb], left)

    def to_other(n, c, block, at):
        ref = gath.at[block, at, own]
        send(ref, ref, gp_s, gp_r, 7 * c + n, other)

    def from_other(n, c, block, at):
        ref = gath.at[block, at, theirs]
        remote(ref, ref, gp_s.at[7 * c + n], gp_r.at[7 * c + n], other).wait_recv()

    def to_x(n, c, block, at, device):
        ref = gath.at[block, at, own]
        send(ref, ref, gx_s, gx_r, 6 * c + n, device)

    def from_x(n, c, block, at, device):
        ref = gath.at[block, at, own]
        remote(ref, ref, gx_s.at[6 * c + n], gx_r.at[6 * c + n], device).wait_recv()

    def error(c):
        t_copies[3, c].wait_recv()
        for n in (2, 3, 4, 5):
            x_copies[n, c].wait_recv()

        @pl.loop(0, half // step_rows, unroll=True)
        def _(r):
            at = pl.ds(pl.multiple_of(c * half + r * step_rows, step_rows), step_rows)
            pred = tp[3, at, own].astype(F32) + trecv[3, at, :].astype(F32)
            pred = pred + fin_p[at, :].astype(F32) + fin_m[at, :].astype(F32)
            miss = pred - teacher[at, :].astype(F32)
            gath[x, at, own] = (miss * jnp.concatenate([weight[at, :]] * (part // DH), axis=1)).astype(BF16)

        qa, qb = quarters(c)
        to_x(0, c, x, qa, right)
        to_x(1, c, x, qb, left)
        to_x(2, c, x, qb, right)
        to_x(3, c, x, qa, left)
        to_other(0, c, x, pl.ds(c * half, half))

    def near_first(c):
        qa, qb = quarters(c)
        from_x(0, c, near_l, qa, left)
        to_x(4, c, near_l, qa, right)
        to_other(1, c, near_l, qa)
        from_x(1, c, near_r, qb, right)
        to_x(5, c, near_r, qb, left)
        to_other(2, c, near_r, qb)

    def near_second(c):
        qa, qb = quarters(c)
        from_x(2, c, near_l, qb, left)
        to_other(3, c, near_l, qb)
        from_x(3, c, near_r, qa, right)
        to_other(4, c, near_r, qa)

    def far_in(c):
        qa, qb = quarters(c)
        from_x(4, c, far, qa, left)
        to_other(5, c, far, qa)
        from_x(5, c, far, qb, right)
        to_other(6, c, far, qb)

    def contract(block, c, lo=0, size=wide, fresh=False):
        at = pl.ds(c * half, half)

        @pl.loop(0, heads * DH // 256, unroll=UC)
        def _(n):
            cols = lanes(n * 256, 256)
            new = dot(
                gath[block, at, lanes(lo, size)],
                w[lanes(n * 256, 256), lanes(block * wide + lo, size)],
                NT,
            )
            acc[at, cols] = new if fresh else acc[at, cols] + new

    def contract_own(c):
        from_other(0, c, x, pl.ds(c * half, half))
        contract(x, c, fresh=True)

    def contract_near(c):
        qa, qb = quarters(c)
        from_other(1, c, near_l, qa)
        from_other(3, c, near_l, qb)
        contract(near_l, c)
        from_other(2, c, near_r, qb)
        from_other(4, c, near_r, qa)
        contract(near_r, c)

    def contract_far(c):
        qa, qb = quarters(c)
        contract(far, c, core * part, part)
        from_other(5, c, far, qa)
        from_other(6, c, far, qb)
        contract(far, c, (1 - core) * part, part)

    first_terms()
    terms(1, 0)
    terms(2, 0)
    right_out(0)
    terms(3, 0)
    left_out(0)
    attend(half, half)
    terms(0, 1)
    relayed(0)
    terms(1, 1)
    far_out(1)
    terms(2, 1)
    right_out(1)
    terms(3, 1)
    left_out(1)
    weigh()
    error(0)
    relayed(1)
    contract_own(0)
    near_first(0)
    near_second(0)
    contract_near(0)
    error(1)
    contract_own(1)
    far_in(0)
    contract_far(0)

    @pl.loop(0, heads, unroll=True)
    def _(h):
        cols = lanes(h * DH, DH)
        g_h = acc[0:half, cols].astype(BF16)
        g[0:half, cols] = g_h
        acc[0:DH, cols] = dot(q[0:half, cols], g_h, TN)

    near_first(1)
    near_second(1)
    contract_near(1)
    far_in(1)
    contract_far(1)

    @pl.loop(0, heads, unroll=True)
    def _(h):
        cols = lanes(h * DH, DH)
        g_h = acc[half:rows, cols].astype(BF16)
        g[half:rows, cols] = g_h
        loc2[head_rows(h), :] = (acc[0:DH, cols] + dot(q[half:rows, cols], g_h, TN)).astype(BF16)

    c_send = peers(True, loc2, got2, c_s, c_r, pr)
    start(c_send)
    got2[mine(pr), :] = loc2[mine(pr), :]

    def block_gradients(lo, hi):
        @pl.loop(lo, hi, unroll=UG)
        def _(h):
            cols = lanes(h * DH, DH)
            (k0, k1), (v0, v1), (q0, q1), (g0, g1) = both(k, cols), both(v, cols), both(q, cols), both(g, cols)
            p = state[head_rows(h), :]
            dq[0:half, cols] = scale * (dot(tri(g0, v0, lower), k0, NN) + dot(g0, p, NT))
            dq[half:rows, cols] = scale * (
                dot(full(g1, v0), k0, NN) + dot(tri(g1, v1, lower), k1, NN) + dot(g1, p, NT)
            )
            dk[0:half, cols] = dot(tri(v0, g0, upper), q0, NN) + dot(full(v0, g1), q1, NN)
            dk[half:rows, cols] = dot(tri(v1, g1, upper), q1, NN)
            dv[0:half, cols] = dot(tri(k0, q0, upper), g0, NN) + dot(full(k0, q1), g1, NN)
            dv[half:rows, cols] = dot(tri(k1, q1, upper), g1, NN)

    block_gradients(0, heads // 2)
    finish_recv(peers(False, loc2, got2, c_s, c_r, pr))
    scan(got2, pre2, True)
    d_send = peers(True, pre2, state2, d_s, d_r, pr)
    start(d_send)
    state2[mine(pr), :] = pre2[mine(pr), :]
    block_gradients(heads // 2, heads)
    finish_send(b_send)
    finish_send(n_send)
    finish_send(sent)
    finish_send(c_send)
    finish_recv(peers(False, pre2, state2, d_s, d_r, pr))
    suffix[...] = state2[...]
    finish_send(d_send)


def gradients(scale, k, v, dq, pk, pv, suffix, dq_out, dk_out, dv_out, dk, dv, sems):
    heads = k.shape[1] // DH
    step = 2
    copies = [pltpu.make_async_copy(dq, dq_out, sems.at[heads])]
    copies[0].start()
    for group in range(heads // step):
        for h in range(group * step, (group + 1) * step):
            cols = slice(h * DH, (h + 1) * DH)
            r = suffix[cols, :]
            dk[:, cols] = scale * (pk[:, cols] + dot(v[:, cols], r, NT))
            dv[:, cols] = scale * (pv[:, cols] + dot(k[:, cols], r, NN))
        span = pl.ds(group * step * DH, step * DH)
        for n, (src, dst) in enumerate(((dk, dk_out), (dv, dv_out))):
            copy = pltpu.make_async_copy(src.at[:, span], dst.at[:, span], sems.at[2 * group + n])
            copy.start()
            copies.append(copy)
    for copy in copies:
        copy.wait()


def on_device(queries, keys, values, teacher, out_weight, valid):
    rows, width = queries.shape
    heads = width // DH
    model = out_weight.shape[1]
    n_ctx = lax.axis_size("ctx")
    n_x = lax.axis_size("head") // 2
    half = rows // 2
    wide = model // n_x
    part = wide // 2
    tokens = float(rows * n_ctx)
    scale = 1.0 / math.sqrt(DH * rows * n_ctx)
    valid_rows = valid.reshape(rows // DH, DH)
    anywhere = pl.BlockSpec(memory_space=pl.ANY)
    vmem = pl.BlockSpec(memory_space=pltpu.VMEM)
    dma = pltpu.SemaphoreType.DMA
    st = lambda: pltpu.VMEM((heads * DH, DH), BF16)
    kept = pltpu.VMEM((rows, width), BF16)
    passed = pl.pallas_call(
        functools.partial(transfer, scale, heads, n_ctx, n_x, tokens),
        name="transfer",
        out_shape=(kept,) * 2 + (pltpu.VMEM((rows, width), F32),) * 3 + (pltpu.VMEM((width, DH), BF16),),
        in_specs=[anywhere] * 5 + [vmem],
        out_specs=(vmem,) * 6,
        scratch_shapes=[
            pltpu.VMEM((rows, width), BF16),
            pltpu.VMEM((rows, part), BF16),
            pltpu.VMEM((width, model), BF16),
            pltpu.VMEM((rows, width), F32),
            pltpu.VMEM((rows, width), BF16),
            pltpu.VMEM((4, rows, wide), BF16),
            pltpu.VMEM((4, rows, part), BF16),
            pltpu.VMEM((2, half // 2, part), BF16),
            pltpu.VMEM((2, half // 2, part), BF16),
            pltpu.VMEM((rows, part), BF16),
            pltpu.VMEM((rows, part), BF16),
            pltpu.VMEM((n_x, rows, wide), BF16),
            pltpu.VMEM((rows, width), F32),
            pltpu.VMEM((rows, width), BF16),
            pltpu.VMEM((rows, DH), F32),
            st(), st(), st(), st(), st(), st(), st(), st(),
            pltpu.VMEM((8, 128), F32),
            pltpu.VMEM((8 * n_ctx, 128), F32),
            dma((5,)),
            dma((n_ctx,)), dma((n_ctx,)), dma((n_ctx,)), dma((n_ctx,)),
            dma((n_ctx,)), dma((n_ctx,)), dma((n_ctx,)), dma((n_ctx,)),
            dma((n_ctx,)), dma((n_ctx,)),
            dma((9,)), dma((9,)), dma((12,)), dma((12,)),
            dma((14,)), dma((14,)), dma((12,)), dma((12,)),
        ],
        compiler_params=pltpu.CompilerParams(
            collective_id=0, has_side_effects=True, vmem_limit_bytes=LIMIT * 1024 * 1024
        ),
    )(queries, keys, values, teacher, out_weight, valid_rows)

    return tuple(pl.pallas_call(
        functools.partial(gradients, scale),
        name="gradients",
        out_shape=(jax.ShapeDtypeStruct((rows, width), F32),) * 3,
        in_specs=[vmem] * 6,
        out_specs=(anywhere,) * 3,
        scratch_shapes=[pltpu.VMEM((rows, width), F32)] * 2 + [dma((heads + 1,))],
        compiler_params=pltpu.CompilerParams(vmem_limit_bytes=16 * 1024 * 1024),
    )(*passed))


def solution(mesh):
    in_specs = (
        P("ctx", "head"),
        P("ctx", "head"),
        P("ctx", "head"),
        P("ctx", "head"),
        P("head", None),
        P("ctx"),
    )
    out_specs = (P("ctx", "head"), P("ctx", "head"), P("ctx", "head"))
    return jax.shard_map(
        on_device, mesh=mesh, in_specs=in_specs, out_specs=out_specs, check_vma=False
    )
```

```python
import functools
import math

import jax
import jax.numpy as jnp
from jax import lax
from jax.experimental import pallas as pl
from jax.experimental.pallas import tpu as pltpu
from jax.sharding import PartitionSpec as P

DH = 128
UT = True
UC = True
UG = 2
CHUNKS = (320, 192)
LIMIT = 54
MESH = pl.DeviceIdType.MESH
F32 = jnp.float32
BF16 = jnp.bfloat16
NT = (((1,), (1,)), ((), ()))
TN = (((0,), (0,)), ((), ()))
NN = (((1,), (0,)), ((), ()))


def dot(a, b, dims):
    return lax.dot_general(a, b, dims, preferred_element_type=F32)


def lanes(start, size):
    return pl.ds(pl.multiple_of(start, 128), size)


def transfer(scale, heads, n_ctx, n_x, tokens,
             q_hbm, k_hbm, v_hbm, teacher_hbm, w_hbm, valid_ref,
             k, v, dq, dk, dv, suffix,
             q, teacher, w, intra, attn, tp, trecv, relay_p, relay_m, fin_p, fin_m,
             gath, acc, g, weight, loc, got, pre, state, loc2, got2, pre2, state2, cnt, cnts,
             in_sem, a_s, a_r, b_s, b_r, c_s, c_r, d_s, d_r, n_s, n_r,
             t_s, t_r, x_s, x_r, gp_s, gp_r, gx_s, gx_r):
    rows = q.shape[0]
    half = rows // 2
    starts = (0, CHUNKS[0])
    wide = w.shape[1] // n_x
    part = wide // 2
    me_c = lax.axis_index("ctx")
    me_h = lax.axis_index("head")
    x, core = me_h // 2, me_h % 2
    right = ((x + 1) % n_x) * 2 + core
    left = ((x + n_x - 1) % n_x) * 2 + core
    other = x * 2 + 1 - core
    pr = heads * DH // n_ctx

    barrier = pltpu.get_barrier_semaphore()
    for d in range(1, n_ctx):
        pl.semaphore_signal(barrier, inc=1, device_id=((me_c + d) % n_ctx, me_h), device_id_type=MESH)
    for h in (other, right, left):
        pl.semaphore_signal(barrier, inc=1, device_id=(me_c, h), device_id_type=MESH)

    loads = [
        pltpu.make_async_copy(src, dst, in_sem.at[i])
        for i, (src, dst) in enumerate(((k_hbm, k), (v_hbm, v), (q_hbm, q), (w_hbm, w), (teacher_hbm, teacher)))
    ]
    for one in loads[:3]:
        one.start()

    n_y = math.isqrt(n_ctx) if math.isqrt(n_ctx) ** 2 == n_ctx else n_ctx
    n_z = n_ctx // n_y
    offsets = sorted(
        ((i, j) for i in range(n_z) for j in range(n_y) if i or j),
        key=lambda o: -min(o[0], n_z - o[0]) - min(o[1], n_y - o[1]),
    )

    def peers(sending, src, dst, ssem, rsem, piece):
        out = []
        for d, (oz, oy) in enumerate(offsets):
            if not sending:
                oz, oy = n_z - oz, n_y - oy
            peer = ((me_c // n_y + oz) % n_z) * n_y + (me_c % n_y + oy) % n_y
            place = me_c if sending else peer
            out.append(pltpu.make_async_remote_copy(
                src_ref=src.at[pl.ds(pl.multiple_of(peer * piece, piece), piece)] if src is not cnt else src,
                dst_ref=dst.at[pl.ds(pl.multiple_of(place * piece, piece), piece)],
                send_sem=ssem.at[d],
                recv_sem=rsem.at[place],
                device_id=(peer, me_h),
                device_id_type=MESH,
            ))
        return out

    def mine(piece):
        return pl.ds(pl.multiple_of(me_c * piece, piece), piece)

    def head_rows(h):
        return pl.ds(pl.multiple_of(h * DH, DH), DH)

    def to_peer(j, src, dst, ssem, rsem):
        return pltpu.make_async_remote_copy(
            src_ref=src.at[j * pr : (j + 1) * pr], dst_ref=dst.at[mine(pr)],
            send_sem=ssem.at[j], recv_sem=rsem.at[me_c],
            device_id=(j, me_h), device_id_type=MESH)

    def scan(loc_ref, got_ref, pre_ref, state_ref, ssem, rsem, ssem2, rsem2, backward):
        total = jnp.zeros((pr, DH), F32)
        order = range(n_ctx - 1, -1, -1) if backward else range(n_ctx)
        for j in order:
            block = slice(j * pr, (j + 1) * pr)
            pre_ref[block, :] = total.astype(BF16)

            @pl.when(me_c != j)
            def _():
                to_peer(j, pre_ref, state_ref, ssem2, rsem2).start()
                pltpu.make_async_remote_copy(
                    src_ref=loc_ref.at[block], dst_ref=got_ref.at[block],
                    send_sem=ssem.at[0], recv_sem=rsem.at[j],
                    device_id=(j, me_h), device_id_type=MESH).wait_recv()

            total = total + got_ref[block, :].astype(F32)
        state_ref[mine(pr), :] = pre_ref[mine(pr), :]

    def finish_scan(pre_ref, state_ref, ssem2, rsem2):
        for j in range(n_ctx):
            @pl.when(me_c != j)
            def _():
                to_peer(j, pre_ref, state_ref, ssem2, rsem2).wait_send()

    def start(copies):
        for one in copies:
            one.start()

    def finish_recv(copies):
        for one in copies:
            one.wait_recv()

    def finish_send(copies):
        for one in copies:
            one.wait_send()

    loads[0].wait()
    loads[1].wait()

    @pl.loop(0, heads, unroll=True)
    def _(h):
        cols = lanes(h * DH, DH)
        loc[head_rows(h), :] = dot(k[:, cols], v[:, cols], TN).astype(BF16)

    loads[3].start()
    loads[4].start()
    cnt[...] = jnp.zeros_like(cnt) + jnp.sum(valid_ref[...].astype(F32))
    pl.semaphore_wait(barrier, n_ctx - 1 + 3)

    a_send = peers(True, loc, got, a_s, a_r, pr)
    start(a_send)
    got[mine(pr), :] = loc[mine(pr), :]
    cnts[mine(8), :] = cnt[...]

    loads[2].wait()
    row = lax.broadcasted_iota(jnp.int32, (half, half), 0)
    col = lax.broadcasted_iota(jnp.int32, (half, half), 1)
    lower = row >= col
    upper = row <= col

    def both(ref, cols):
        return ref[0:half, cols], ref[half:rows, cols]

    def full(a, b):
        return dot(a, b, NT).astype(BF16)

    def tri(a, b, mask):
        return jnp.where(mask, dot(a, b, NT), 0.0).astype(BF16)

    @pl.loop(0, heads, unroll=2)
    def _(h):
        cols = lanes(h * DH, DH)
        (k0, k1), (v0, v1), (q0, q1) = both(k, cols), both(v, cols), both(q, cols)
        intra[0:half, cols] = dot(tri(q0, k0, lower), v0, NN)
        intra[half:rows, cols] = dot(full(q1, k0), v0, NN) + dot(tri(q1, k1, lower), v1, NN)

    scan(loc, got, pre, state, a_s, a_r, b_s, b_r, False)
    n_send = peers(True, cnt, cnts, n_s, n_r, 8)
    start(n_send)
    finish_send(a_send)
    loads[3].wait()
    loads[4].wait()
    finish_recv(peers(False, pre, state, b_s, b_r, pr))

    def weigh():
        finish_recv(peers(False, cnt, cnts, n_s, n_r, 8))
        count = cnts[0:8, :]
        for j in range(1, n_ctx):
            count = count + cnts[j * 8 : j * 8 + 8, :]
        factor = (tokens / count)[0:1, :]
        diagonal = row[0:DH, 0:DH] == col[0:DH, 0:DH]
        for j in range(rows // DH):
            column = jnp.sum(jnp.where(diagonal, valid_ref[j : j + 1, :].astype(F32), 0.0), axis=1, keepdims=True)
            weight[j * DH : (j + 1) * DH, :] = column * factor

    def attend(base, size):
        at = pl.ds(base, size)

        @pl.loop(0, heads, unroll=True)
        def _(h):
            cols = lanes(h * DH, DH)
            carried = dot(q[at, cols], state[head_rows(h), :], NN)
            attn[at, cols] = (scale * (intra[at, cols] + carried)).astype(BF16)

    def remote(src, dst, ssem, rsem, device):
        return pltpu.make_async_remote_copy(
            src_ref=src, dst_ref=dst, send_sem=ssem, recv_sem=rsem,
            device_id=(me_c, device), device_id_type=MESH)

    own = lanes(core * part, part)
    theirs = lanes((1 - core) * part, part)
    step_rows = 32
    sent = []

    def send(src, dst, ssem, rsem, n, device):
        copy = remote(src, dst, ssem.at[n], rsem.at[n], device)
        copy.start()
        sent.append(copy)
        return copy

    def quarters(c):
        size = CHUNKS[c] // 2
        return pl.ds(starts[c], size), pl.ds(starts[c] + size, size)

    def chunk(c):
        return pl.ds(starts[c], CHUNKS[c])

    near_r, near_l, far = (x + 1) % n_x, (x + n_x - 1) % n_x, (x + 2) % n_x
    targets = [far, near_r, near_l, x]
    t_copies, x_copies = {}, {}

    def some_terms(at, here):
        lo = 0
        while lo < part:
            size = min(256, part - lo)
            tp[0, at, lanes(here + lo, size)] = dot(
                attn[at, :], w[:, lanes(far * wide + here + lo, size)], NN).astype(BF16)
            lo += size

    def first_terms():
        parts = quarters(0)
        copies = []
        for n, at in enumerate(parts):
            attend(n * CHUNKS[0] // 2, CHUNKS[0] // 2)
            some_terms(at, (1 - core) * part)
            copies.append(send(tp.at[0, at, theirs], trecv.at[0, at, :], t_s, t_r, (0, 8)[n], other))
        some_terms(chunk(0), core * part)
        for n, (at, relay, device) in enumerate(zip(parts, (relay_p, relay_m), (right, left))):
            copies[n].wait_recv()
            add_rows(0, n * CHUNKS[0] // 2, CHUNKS[0] // 2)
            send_x(n, 0, tp.at[0, at, own], relay.at[at], device)

    def terms(i, c):
        at = chunk(c)
        base = targets[i] * wide

        @pl.loop(0, wide // 256, unroll=UT)
        def _(n):
            tp[i, at, lanes(n * 256, 256)] = dot(attn[at, :], w[:, lanes(base + n * 256, 256)], NN).astype(BF16)

        t_copies[i, c] = send(tp.at[i, at, theirs], trecv.at[i, at, :], t_s, t_r, 4 * c + i, other)

    def add_chip(i, c):
        t_copies[i, c].wait_recv()
        add_rows(i, starts[c], CHUNKS[c])

    def add_rows(i, base, size):
        @pl.loop(0, size // step_rows, unroll=True)
        def _(r):
            at = pl.ds(pl.multiple_of(base + r * step_rows, step_rows), step_rows)
            tp[i, at, own] = (tp[i, at, own].astype(F32) + trecv[i, at, :].astype(F32)).astype(BF16)

    def add_relay(i, rel, c, base):
        @pl.loop(0, CHUNKS[c] // 2 // step_rows, unroll=True)
        def _(r):
            off = pl.multiple_of(r * step_rows, step_rows)
            at = pl.ds(base + off, step_rows)
            tp[i, at, own] = (tp[i, at, own].astype(F32) + rel[pl.ds(base + off, step_rows), :].astype(F32)).astype(BF16)

    def send_x(n, c, src, dst, device):
        x_copies[n, c] = send(src, dst, x_s, x_r, 6 * c + n, device)

    def far_out(c):
        qa, qb = quarters(c)
        add_chip(0, c)
        send_x(0, c, tp.at[0, qa, own], relay_p.at[qa], right)
        send_x(1, c, tp.at[0, qb, own], relay_m.at[qb], left)

    def right_out(c):
        qa, qb = quarters(c)
        add_chip(1, c)
        send_x(2, c, tp.at[1, qb, own], fin_p.at[qb], right)

    def left_out(c):
        qa, qb = quarters(c)
        add_chip(2, c)
        send_x(3, c, tp.at[2, qa, own], fin_m.at[qa], left)

    def relayed(c):
        qa, qb = quarters(c)
        x_copies[0, c].wait_recv()
        add_relay(1, relay_p, c, starts[c])
        send_x(4, c, tp.at[1, qa, own], fin_p.at[qa], right)
        x_copies[1, c].wait_recv()
        add_relay(2, relay_m, c, starts[c] + CHUNKS[c] // 2)
        send_x(5, c, tp.at[2, qb, own], fin_m.at[qb], left)

    def to_other(n, c, block, at):
        ref = gath.at[block, at, own]
        send(ref, ref, gp_s, gp_r, 7 * c + n, other)

    def from_other(n, c, block, at):
        ref = gath.at[block, at, theirs]
        remote(ref, ref, gp_s.at[7 * c + n], gp_r.at[7 * c + n], other).wait_recv()

    def to_x(n, c, block, at, device):
        ref = gath.at[block, at, own]
        send(ref, ref, gx_s, gx_r, 6 * c + n, device)

    def from_x(n, c, block, at, device):
        ref = gath.at[block, at, own]
        remote(ref, ref, gx_s.at[6 * c + n], gx_r.at[6 * c + n], device).wait_recv()

    def error(c):
        t_copies[3, c].wait_recv()
        for n in (2, 3, 4, 5):
            x_copies[n, c].wait_recv()

        @pl.loop(0, CHUNKS[c] // step_rows, unroll=True)
        def _(r):
            at = pl.ds(pl.multiple_of(starts[c] + r * step_rows, step_rows), step_rows)
            pred = tp[3, at, own].astype(F32) + trecv[3, at, :].astype(F32)
            pred = pred + fin_p[at, :].astype(F32) + fin_m[at, :].astype(F32)
            miss = pred - teacher[at, :].astype(F32)
            gath[x, at, own] = (miss * jnp.concatenate([weight[at, :]] * (part // DH), axis=1)).astype(BF16)

        qa, qb = quarters(c)
        to_x(0, c, x, qa, right)
        to_x(1, c, x, qb, left)
        to_x(2, c, x, qb, right)
        to_x(3, c, x, qa, left)
        to_other(0, c, x, chunk(c))

    def near_first(c):
        qa, qb = quarters(c)
        from_x(0, c, near_l, qa, left)
        to_x(4, c, near_l, qa, right)
        to_other(1, c, near_l, qa)
        from_x(1, c, near_r, qb, right)
        to_x(5, c, near_r, qb, left)
        to_other(2, c, near_r, qb)

    def near_second(c):
        qa, qb = quarters(c)
        from_x(2, c, near_l, qb, left)
        to_other(3, c, near_l, qb)
        from_x(3, c, near_r, qa, right)
        to_other(4, c, near_r, qa)

    def far_in(c):
        qa, qb = quarters(c)
        from_x(4, c, far, qa, left)
        to_other(5, c, far, qa)
        from_x(5, c, far, qb, right)
        to_other(6, c, far, qb)

    def contract(block, c, lo=0, size=wide, fresh=False):
        at = chunk(c)

        @pl.loop(0, heads * DH // 256, unroll=UC)
        def _(n):
            cols = lanes(n * 256, 256)
            new = dot(
                gath[block, at, lanes(lo, size)],
                w[lanes(n * 256, 256), lanes(block * wide + lo, size)],
                NT,
            )
            acc[at, cols] = new if fresh else acc[at, cols] + new

    def contract_own(c):
        from_other(0, c, x, chunk(c))
        contract(x, c, fresh=True)

    def contract_near(c):
        qa, qb = quarters(c)
        from_other(1, c, near_l, qa)
        from_other(3, c, near_l, qb)
        contract(near_l, c)
        from_other(2, c, near_r, qb)
        from_other(4, c, near_r, qa)
        contract(near_r, c)

    def contract_far(c):
        qa, qb = quarters(c)
        contract(far, c, core * part, part)
        from_other(5, c, far, qa)
        from_other(6, c, far, qb)
        contract(far, c, (1 - core) * part, part)

    first_terms()
    terms(1, 0)
    terms(2, 0)
    right_out(0)
    terms(3, 0)
    left_out(0)
    attend(starts[1], CHUNKS[1])
    terms(0, 1)
    relayed(0)
    terms(1, 1)
    far_out(1)
    terms(2, 1)
    right_out(1)
    terms(3, 1)
    left_out(1)
    weigh()
    error(0)
    relayed(1)
    contract_own(0)
    near_first(0)
    near_second(0)
    contract_near(0)
    error(1)
    contract_own(1)
    far_in(0)
    contract_far(0)

    @pl.loop(0, heads, unroll=True)
    def _(h):
        cols = lanes(h * DH, DH)
        g_h = acc[0:CHUNKS[0], cols].astype(BF16)
        g[0:CHUNKS[0], cols] = g_h
        acc[0:DH, cols] = dot(q[0:CHUNKS[0], cols], g_h, TN)

    near_first(1)
    near_second(1)
    contract_near(1)
    far_in(1)
    contract_far(1)

    @pl.loop(0, heads, unroll=True)
    def _(h):
        cols = lanes(h * DH, DH)
        g_h = acc[CHUNKS[0]:rows, cols].astype(BF16)
        g[CHUNKS[0]:rows, cols] = g_h
        loc2[head_rows(h), :] = (acc[0:DH, cols] + dot(q[CHUNKS[0]:rows, cols], g_h, TN)).astype(BF16)

    c_send = peers(True, loc2, got2, c_s, c_r, pr)
    start(c_send)
    got2[mine(pr), :] = loc2[mine(pr), :]

    def block_gradients(lo, hi):
        @pl.loop(lo, hi, unroll=UG)
        def _(h):
            cols = lanes(h * DH, DH)
            (k0, k1), (v0, v1), (q0, q1), (g0, g1) = both(k, cols), both(v, cols), both(q, cols), both(g, cols)
            p = state[head_rows(h), :]
            dq[0:half, cols] = scale * (dot(tri(g0, v0, lower), k0, NN) + dot(g0, p, NT))
            dq[half:rows, cols] = scale * (
                dot(full(g1, v0), k0, NN) + dot(tri(g1, v1, lower), k1, NN) + dot(g1, p, NT)
            )
            dk[0:half, cols] = dot(tri(v0, g0, upper), q0, NN) + dot(full(v0, g1), q1, NN)
            dk[half:rows, cols] = dot(tri(v1, g1, upper), q1, NN)
            dv[0:half, cols] = dot(tri(k0, q0, upper), g0, NN) + dot(full(k0, q1), g1, NN)
            dv[half:rows, cols] = dot(tri(k1, q1, upper), g1, NN)

    block_gradients(0, heads // 2)
    scan(loc2, got2, pre2, state2, c_s, c_r, d_s, d_r, True)
    block_gradients(heads // 2, heads)
    finish_scan(pre, state, b_s, b_r)
    finish_send(n_send)
    finish_send(sent)
    finish_send(c_send)
    finish_recv(peers(False, pre2, state2, d_s, d_r, pr))
    suffix[...] = state2[...]
    finish_scan(pre2, state2, d_s, d_r)


def gradients(scale, k, v, dq, pk, pv, suffix, dq_out, dk_out, dv_out, dk, dv, sems):
    heads = k.shape[1] // DH
    step = 2
    copies = [pltpu.make_async_copy(dq, dq_out, sems.at[heads])]
    copies[0].start()
    for group in range(heads // step):
        for h in range(group * step, (group + 1) * step):
            cols = slice(h * DH, (h + 1) * DH)
            r = suffix[cols, :]
            dk[:, cols] = scale * (pk[:, cols] + dot(v[:, cols], r, NT))
            dv[:, cols] = scale * (pv[:, cols] + dot(k[:, cols], r, NN))
        span = pl.ds(group * step * DH, step * DH)
        for n, (src, dst) in enumerate(((dk, dk_out), (dv, dv_out))):
            copy = pltpu.make_async_copy(src.at[:, span], dst.at[:, span], sems.at[2 * group + n])
            copy.start()
            copies.append(copy)
    for copy in copies:
        copy.wait()


def on_device(queries, keys, values, teacher, out_weight, valid):
    rows, width = queries.shape
    heads = width // DH
    model = out_weight.shape[1]
    n_ctx = lax.axis_size("ctx")
    n_x = lax.axis_size("head") // 2
    wide = model // n_x
    part = wide // 2
    tokens = float(rows * n_ctx)
    scale = 1.0 / math.sqrt(DH * rows * n_ctx)
    valid_rows = valid.reshape(rows // DH, DH)
    anywhere = pl.BlockSpec(memory_space=pl.ANY)
    vmem = pl.BlockSpec(memory_space=pltpu.VMEM)
    dma = pltpu.SemaphoreType.DMA
    st = lambda: pltpu.VMEM((heads * DH, DH), BF16)
    kept = pltpu.VMEM((rows, width), BF16)
    passed = pl.pallas_call(
        functools.partial(transfer, scale, heads, n_ctx, n_x, tokens),
        name="transfer",
        out_shape=(kept,) * 2 + (pltpu.VMEM((rows, width), F32),) * 3 + (pltpu.VMEM((width, DH), BF16),),
        in_specs=[anywhere] * 5 + [vmem],
        out_specs=(vmem,) * 6,
        scratch_shapes=[
            pltpu.VMEM((rows, width), BF16),
            pltpu.VMEM((rows, part), BF16),
            pltpu.VMEM((width, model), BF16),
            pltpu.VMEM((rows, width), F32),
            pltpu.VMEM((rows, width), BF16),
            pltpu.VMEM((4, rows, wide), BF16),
            pltpu.VMEM((4, rows, part), BF16),
            pltpu.VMEM((rows, part), BF16),
            pltpu.VMEM((rows, part), BF16),
            pltpu.VMEM((rows, part), BF16),
            pltpu.VMEM((rows, part), BF16),
            pltpu.VMEM((n_x, rows, wide), BF16),
            pltpu.VMEM((rows, width), F32),
            pltpu.VMEM((rows, width), BF16),
            pltpu.VMEM((rows, DH), F32),
            st(), st(), st(), st(), st(), st(), st(), st(),
            pltpu.VMEM((8, 128), F32),
            pltpu.VMEM((8 * n_ctx, 128), F32),
            dma((5,)),
            dma((n_ctx,)), dma((n_ctx,)), dma((n_ctx,)), dma((n_ctx,)),
            dma((n_ctx,)), dma((n_ctx,)), dma((n_ctx,)), dma((n_ctx,)),
            dma((n_ctx,)), dma((n_ctx,)),
            dma((9,)), dma((9,)), dma((12,)), dma((12,)),
            dma((14,)), dma((14,)), dma((12,)), dma((12,)),
        ],
        compiler_params=pltpu.CompilerParams(
            collective_id=0, has_side_effects=True, vmem_limit_bytes=LIMIT * 1024 * 1024
        ),
    )(queries, keys, values, teacher, out_weight, valid_rows)

    return tuple(pl.pallas_call(
        functools.partial(gradients, scale),
        name="gradients",
        out_shape=(jax.ShapeDtypeStruct((rows, width), F32),) * 3,
        in_specs=[vmem] * 6,
        out_specs=(anywhere,) * 3,
        scratch_shapes=[pltpu.VMEM((rows, width), F32)] * 2 + [dma((heads + 1,))],
        compiler_params=pltpu.CompilerParams(vmem_limit_bytes=16 * 1024 * 1024),
    )(*passed))


def solution(mesh):
    in_specs = (
        P("ctx", "head"),
        P("ctx", "head"),
        P("ctx", "head"),
        P("ctx", "head"),
        P("head", None),
        P("ctx"),
    )
    out_specs = (P("ctx", "head"), P("ctx", "head"), P("ctx", "head"))
    return jax.shard_map(
        on_device, mesh=mesh, in_specs=in_specs, out_specs=out_specs, check_vma=False
    )
```
